128 devices in a mesh: inline: 16 (over x, y), crosslin: 8 (over z, core).
Axes of the slice: x: 4, y: 4, z: 4, core: 2. Of those that a mesh axis runs over, the one named last changes fastest.
Arguments:
- traces: float32 [16384, 4, 1024], P(('inline', 'crosslin')), may hold values from -6 to 6
- destination: int32 [16384, 1], P(('inline', 'crosslin')), may hold values from 0 to 127; in each aligned block of 128 rows (0 to 127, 128 to 255, ...) at most 2 rows name the same one
- bin_index: int32 [16384, 4], P(('inline', 'crosslin')), may hold values from 0 to 1023
- dip_inline: int32 [512, 256], P('inline', 'crosslin'), may hold values from -2 to 2
- dip_cross: int32 [512, 256], P('inline', 'crosslin'), may hold values from -2 to 2
Outputs:
- smoothed: float32 [512, 256, 1024], P('inline', 'crosslin')
The draws below stay inside these ranges and needn't reach their ends.
Inputs may be any that keep to these rules, and one draw needn't show every extreme that they name: `destination`: at most 2 of one device's blocks name the same tile, and that many are reached.
All inputs are finite; a program needn't handle non-finite values.
Results may differ from the reference program's by a relative error of at most 0.00009.
Values sent between devices are 32-bit elements; how exact they have to be, the bound alone decides.
A program may use at most 64 MiB of HBM per device.

```python
import math
import jax
import jax.numpy as jnp
import numpy as np
from jax import lax

NS = 1024
BT = 4
SB = 128
BI = 32
BX = 32
HALF = 7
DMAX = 2
CAP = 2
BINS = 1024
BLOCKS = 16384
NBI = 512
NBX = 256
N_CROSSLIN = 8
DEVICES = 128


def place_ends(entries, stream_key, low, top_value):
    shape = entries.shape
    index_at = [jax.random.randint(jax.random.fold_in(stream_key, axis), (), 0, shape[axis]) for axis in range(len(shape))]
    entries = entries.at[tuple(index_at)].set(low)
    longest = shape.index(max(shape))
    index_at[longest] = (index_at[longest] + 1) % shape[longest]
    return entries.at[tuple(index_at)].set(top_value)


def level_of(rng, shape, cuts, low, largest):
    factor_of = 1.0
    for axis_at, parts in cuts:
        steps = jax.random.uniform(jax.random.fold_in(jax.random.fold_in(rng, 6), axis_at), (parts,), jnp.float32, low / len(cuts), largest / len(cuts))
        factor_of = factor_of * jnp.repeat(jnp.exp(steps), shape[axis_at] // parts).reshape((-1,) + (1,) * (len(shape) - 1 - axis_at))
    return factor_of


def shared_out(key, own, number, rows, number_of, top, limit, slope):
    order = jax.random.permutation(key, number_of)
    heavy_load, ordinary = portions_of(number_of, rows * top, limit, slope, True), portions_of(number_of, rows * top, limit, slope, False)
    places = jnp.arange(number_of)

    def named(lengths, turn):
        used = int((lengths > 0).sum())
        fixed = max(1, used // 4)
        moved = fixed + (places - fixed + turn * (used - fixed)) % max(1, number_of - fixed)
        return jnp.zeros((number_of,), jnp.int32).at[order[jnp.where(places < fixed, places, moved)]].set(jnp.asarray(lengths, jnp.int32))

    lengths = jnp.where(number % 4 == 0, named(heavy_load, number // 4), named(ordinary, number - number // 4 - 1))
    mixed = jax.random.permutation(jax.random.fold_in(own, 3), number_of)
    giver, sink = mixed[0:number_of // 2 * 2:2], mixed[1:number_of // 2 * 2:2]
    room = jnp.minimum(lengths[giver] - 1, limit - lengths[sink]) // 2
    room = jnp.where((giver == order[0]) | (sink == order[0]) | (lengths[sink] == 0), 0, jnp.maximum(room, 0))
    moved = jax.random.randint(jax.random.fold_in(own, 4), (number_of // 2,), 0, 1 << 20) % (room + 1)
    lengths = lengths.at[giver].add(-moved).at[sink].add(moved)
    members = jnp.searchsorted(jnp.cumsum(lengths), jnp.arange(rows * top), side="right").astype(jnp.int32)
    table = members.reshape(top, rows).T
    table = table[jax.random.permutation(jax.random.fold_in(own, 1), rows)]
    turn = jax.random.randint(jax.random.fold_in(own, 2), (rows, 1), 0, top)
    return jnp.take_along_axis(table, (jnp.arange(top)[None, :] + turn) % top, axis=1)


def portions_of(amount, total, bound, slope, full):
    portions = [(1 << 20) // math.isqrt(grade ** slope) + 1 for grade in range(1, amount + 1)]
    largest = bound if full else min(bound, max(-(-total // amount), total * portions[0] // sum(portions)))
    least = 1 if total - largest >= amount - 1 else 0
    counts, surplus = [largest] + [least] * (amount - 1), total - largest - least * (amount - 1)
    while surplus > 0:
        candidates = [i for i in range(1, amount) if counts[i] < largest] or [i for i in range(1, amount) if counts[i] < bound]
        mass, budget = sum([portions[i] for i in candidates]), surplus
        for i in candidates:
            more = min(bound - counts[i], max(1, budget * portions[i] // mass), surplus)
            counts[i] = counts[i] + more
            surplus = surplus - more
    return np.array(counts)


def centred(key, shape, scale, limit, cuts=(), held_as=jnp.bfloat16):
    array = jax.random.normal(key, shape, jnp.float32) * scale
    if len(cuts) > 0:
        array = level_of(key, shape, cuts, -0.22, 0.18) * array
    return jnp.clip(array, min=-limit, max=limit).astype(held_as)


def setup_inputs(seed: int = 0) -> dict:
    key_list = jax.random.split(jax.random.key(seed), 6)
    traces = centred(key_list[0], (BLOCKS, BT, NS), 1.0, 6.0, ((0, 128),), jnp.float32)
    destination_keys = jax.random.split(jax.random.fold_in(key_list[1], 1), BLOCKS // SB)
    destination_turns = jax.random.permutation(jax.random.fold_in(key_list[1], 3), BLOCKS // SB)
    destination = jax.vmap(lambda own, number: shared_out(jax.random.fold_in(key_list[1], 2), own, number, SB, DEVICES, 1, CAP, 1))(destination_keys, destination_turns).reshape((BLOCKS, 1))
    bin_index = place_ends(jax.random.randint(key_list[2], (BLOCKS, BT), 0, BINS), jax.random.fold_in(key_list[2], 1), 0, BINS - 1).astype(jnp.int32)
    dip_inline = place_ends(jax.random.randint(key_list[3], (NBI, NBX), -DMAX, DMAX + 1), jax.random.fold_in(key_list[3], 1), -DMAX, DMAX).astype(jnp.int32)
    dip_cross = place_ends(jax.random.randint(key_list[4], (NBI, NBX), -DMAX, DMAX + 1), jax.random.fold_in(key_list[4], 1), -DMAX, DMAX).astype(jnp.int32)
    return dict(traces=traces, destination=destination, bin_index=bin_index, dip_inline=dip_inline, dip_cross=dip_cross)


def steer(padded, dip_index, along_dim):
    margin = HALF * DMAX
    samples = padded.shape[-1] - 2 * margin
    extent = padded.shape[along_dim] - 2 * HALF
    result = jnp.zeros(dip_index.shape + (samples,), jnp.float32)
    for dip_value in range(-DMAX, DMAX + 1):
        running = jnp.zeros(dip_index.shape + (samples,), jnp.float32)
        for offset in range(-HALF, HALF + 1):
            weight = (HALF + 1 - abs(offset)) / float((HALF + 1) ** 2)
            shifted = lax.slice_in_dim(padded, HALF + offset, HALF + offset + extent, axis=along_dim)
            begin = margin + dip_value * offset
            shifted = shifted[..., begin:begin + samples]
            running = running + weight * shifted
        result = jnp.where((dip_index == dip_value)[..., None], running, result)
    return result


def pad_grid(gridded, along_dim):
    margin = HALF * DMAX
    widths = [(0, 0), (0, 0), (margin, margin)]
    widths[along_dim] = (HALF, HALF)
    return jnp.pad(gridded, widths)


def reference(traces, destination, bin_index, dip_inline, dip_cross):
    target = destination[:, 0]
    row_index = (target // N_CROSSLIN)[:, None] * BI + bin_index // BX
    col_index = (target % N_CROSSLIN)[:, None] * BX + bin_index % BX
    segment = (row_index * NBX + col_index).reshape(-1).astype(jnp.int32)
    samples = traces.shape[-1]
    summed = jax.ops.segment_sum(traces.reshape(-1, samples), segment, num_segments=NBI * NBX)
    fold_count = jax.ops.segment_sum(jnp.ones(segment.shape, jnp.float32), segment, num_segments=NBI * NBX)
    stacked = (summed / jnp.maximum(fold_count, 1.0)[:, None]).reshape(NBI, NBX, samples)
    first_pass = steer(pad_grid(stacked, 0), dip_inline, 0)
    second_pass = steer(pad_grid(first_pass, 1), dip_cross, 1)
    return steer(pad_grid(second_pass, 0), dip_inline, 0)
```

```python
import functools

import jax
import jax.numpy as jnp
from jax import lax
from jax.experimental import pallas as pl
from jax.experimental.pallas import tpu as pltpu
from jax.sharding import PartitionSpec as P

HALF = 7
DMAX = 2
DIPS = 2 * DMAX + 1
TILE = 32
BINS = TILE * TILE
DEV = 128
SUB, LANE = 8, 128
SPAN = 40
GROUP = 8
ROOM = BINS + GROUP
PAY = 72
HALO = HALF * TILE

VM = pl.BlockSpec(memory_space=pltpu.VMEM)
SM = pl.BlockSpec(memory_space=pltpu.SMEM)
HB = pl.BlockSpec(memory_space=pl.ANY)


def params():
    return pltpu.CompilerParams(vmem_limit_bytes=60 << 20)


def pack_kernel(dest, bins, x, out, scr, z, brow, cnt, sem, bsem):
    for tr in range(4):
        for j in range(8):
            z[pl.ds(j * 128, 128), :] = x[pl.ds(j * 4 + tr, 128, stride=32), :].T
        for ti in range(SUB):
            scr[pl.ds(tr * 8 + ti, 128, stride=32), :] = z[pl.ds(ti, 128, stride=8), :].T
    brow[...] = jnp.full((DEV, 1, LANE), float(BINS), jnp.float32)

    def clear(i, _):
        cnt[i] = 0
        return 0

    lax.fori_loop(0, DEV, clear, 0, unroll=8)
    lane = lax.broadcasted_iota(jnp.int32, (1, LANE), 1)

    def place(b, _):
        t = dest[b]
        rank = cnt[t]
        cnt[t] = rank + 1
        pltpu.make_async_copy(
            scr.at[pl.ds(b * 32, 32)], out.at[t, pl.ds(rank * 32, 32)], sem
        ).start()
        row = brow[t]
        for q in range(4):
            row = jnp.where(lane == rank * 4 + q, bins[b * 4 + q].astype(jnp.float32), row)
        brow[t] = row
        return 0

    lax.fori_loop(0, DEV, place, 0)
    copy = pltpu.make_async_copy(brow, out.at[:, pl.ds(64, 1)], bsem)
    copy.start()
    pltpu.make_async_copy(scr, scr, sem).wait()
    copy.wait()


def pack(dest, bins, x):
    return pl.pallas_call(
        pack_kernel,
        out_shape=jax.ShapeDtypeStruct((DEV, PAY, LANE), jnp.float32),
        in_specs=[SM, SM, VM],
        out_specs=HB,
        scratch_shapes=[
            pltpu.VMEM((4096, LANE), jnp.float32),
            pltpu.VMEM((1024, LANE), jnp.float32),
            pltpu.VMEM((DEV, 1, LANE), jnp.float32),
            pltpu.SMEM((DEV,), jnp.int32),
            pltpu.SemaphoreType.DMA,
            pltpu.SemaphoreType.DMA,
        ],
        compiler_params=params(),
        name="pack",
    )(dest, bins, x)


def lists_kernel(dips, table, count):
    for m in range(2):
        for d in range(DIPS):
            count[m * DIPS + d] = 0

        def add(i, _):
            at = m * DIPS + dips[m * BINS + i] + DMAX
            n = count[at]
            table[at * ROOM + n] = i
            count[at] = n + 1
            return 0

        lax.fori_loop(0, BINS, add, 0, unroll=4)
        for d in range(DIPS):
            n = count[m * DIPS + d]
            for u in range(GROUP):
                table[(m * DIPS + d) * ROOM + n + u] = BINS


def make_lists(dips):
    return pl.pallas_call(
        lists_kernel,
        out_shape=(
            jax.ShapeDtypeStruct((2 * DIPS * ROOM,), jnp.int32),
            jax.ShapeDtypeStruct((2 * DIPS,), jnp.int32),
        ),
        in_specs=[SM],
        out_specs=(SM, SM),
        compiler_params=params(),
        cost_estimate=pl.CostEstimate(flops=0, bytes_accessed=60 << 20, transcendentals=0),
        name="lists",
    )(dips)


def bin_kernel(bins, scale, x, out, head, tail, *sums):
    zero = jnp.zeros((SUB, LANE), jnp.float32)

    def clear(i, _):
        for s in sums:
            s[i] = zero
        return 0

    lax.fori_loop(0, BINS, clear, 0, unroll=8)

    def add(i, _):
        for slot in range(2):
            for tr in range(4):
                b = bins[i * 8 + slot * 4 + tr]
                sums[tr][b] += x[i, pl.ds(slot * 32 + tr * 8, 8), :]
        return 0

    lax.fori_loop(0, DEV, add, 0, unroll=2)

    def finish(i, _):
        out[i] = ((sums[0][i] + sums[1][i]) + (sums[2][i] + sums[3][i])) * scale[i]
        return 0

    lax.fori_loop(0, BINS, finish, 0, unroll=8)
    head[...] = out[pl.ds(0, HALO)]
    tail[...] = out[pl.ds(BINS - HALO, HALO)]


FULL = jax.ShapeDtypeStruct((BINS, SUB, LANE), jnp.float32)
EDGE = jax.ShapeDtypeStruct((HALO, SUB, LANE), jnp.float32)


def put_bins(bins, scale, x):
    return pl.pallas_call(
        bin_kernel,
        out_shape=(FULL, EDGE, EDGE),
        in_specs=[SM, SM, VM],
        out_specs=(VM, VM, VM),
        scratch_shapes=[pltpu.VMEM((BINS + 1, SUB, LANE), jnp.float32) for _ in range(4)],
        compiler_params=params(),
        name="put_bins",
    )(bins, scale, x)


def widen(ext, row, x, lane):
    ext[pl.ds(row + 16, 8), :] = x
    ext[pl.ds(row + 24, 8), :] = jnp.where(lane < 127, pltpu.roll(x, 127, 1), 0.0)
    ext[pl.ds(row + 32, 8), :] = jnp.where(lane < 126, pltpu.roll(x, 126, 1), 0.0)
    ext[pl.ds(row + 8, 8), :] = jnp.where(lane >= 1, pltpu.roll(x, 1, 1), 0.0)
    ext[pl.ds(row, 8), :] = jnp.where(lane >= 2, pltpu.roll(x, 2, 1), 0.0)


def row_margins(ext, own, lo, hi):
    lane = lax.broadcasted_iota(jnp.int32, (SUB, LANE), 1)

    def inner(i, _):
        widen(ext, pl.multiple_of((i + HALO) * SPAN, 8), own[i], lane)
        return 0

    lax.fori_loop(0, BINS, inner, 0, unroll=8)

    def outer(i, _):
        widen(ext, pl.multiple_of(i * SPAN, 8), lo[i], lane)
        widen(ext, pl.multiple_of((i + HALO + BINS) * SPAN, 8), hi[i], lane)
        return 0

    lax.fori_loop(0, HALO, outer, 0, unroll=4)


WIDE = TILE + 2 * HALF


def col_margins(ext, own, lo, hi):
    lane = lax.broadcasted_iota(jnp.int32, (SUB, LANE), 1)

    def row(r, _):
        def inner(c, _):
            widen(ext, pl.multiple_of((r * WIDE + HALF + c) * SPAN, 8), own[r * TILE + c], lane)
            return 0

        lax.fori_loop(0, TILE, inner, 0, unroll=8)
        for c in range(HALF):
            widen(ext, pl.multiple_of((r * WIDE + c) * SPAN, 8), lo[r * HALF + c], lane)
            widen(
                ext, pl.multiple_of((r * WIDE + HALF + TILE + c) * SPAN, 8), hi[r * HALF + c], lane
            )
        return 0

    lax.fori_loop(0, TILE, row, 0)


def steer(table, count, which, ext, along_rows, write):
    stride = TILE if along_rows else 1
    for d in range(-DMAX, DMAX + 1):
        at = which * DIPS + d + DMAX
        base0 = 16 - HALF * d

        def group(g, _):
            for u in range(GROUP):
                b = table[at * ROOM + g * GROUP + u]
                first = b if along_rows else b + 2 * HALF * (b >> 5)
                view = ext.at[pl.ds(pl.multiple_of(first * SPAN, 8), 14 * stride * SPAN + SPAN)]

                def tap(k):
                    return view[pl.ds(base0 + (k + HALF) * (stride * SPAN + d), 8), :]

                total = tap(0) * (1.0 / 8.0)
                for k in range(1, HALF + 1):
                    total = total + (tap(k) + tap(-k)) * ((HALF + 1 - k) / 64.0)
                write(b, total)
            return 0

        lax.fori_loop(0, (count[at] + GROUP - 1) // GROUP, group, 0)


def first_kernel(table, count, own, lo, hi, out, left, right, ext, acc):
    row_margins(ext, own, lo, hi)

    def write(b, v):
        acc[b] = v

    steer(table, count, 0, ext, True, write)
    out[...] = acc[pl.ds(0, BINS)]

    def cut(r, _):
        for c in range(HALF):
            left[r * HALF + c] = acc[r * TILE + c]
            right[r * HALF + c] = acc[r * TILE + TILE - HALF + c]
        return 0

    lax.fori_loop(0, TILE, cut, 0)


def second_kernel(table, count, own, lo, hi, out, head, tail, ext, acc):
    col_margins(ext, own, lo, hi)

    def write(b, v):
        acc[b] = v

    steer(table, count, 1, ext, False, write)
    out[...] = acc[pl.ds(0, BINS)]
    head[...] = acc[pl.ds(0, HALO)]
    tail[...] = acc[pl.ds(BINS - HALO, HALO)]


def third_kernel(table, count, own, lo, hi, out, ext, acc, z):
    row_margins(ext, own, lo, hi)

    def write(b, v):
        acc[pl.ds(pl.multiple_of(b * 8, 8), 8), :] = v

    steer(table, count, 0, ext, True, write)

    def natural(i, _):
        for ti in range(SUB):
            z[pl.ds(ti, 128, stride=8), :] = acc[pl.ds(i * 1024 + ti, 128, stride=8), :].T
        for j in range(8):
            out[pl.ds(i * 4, 4), :, pl.ds(j * 128, 128)] = (
                z[pl.ds(j * 128, 128), :].T.reshape(4, 32, 128)
            )
        return 0

    lax.fori_loop(0, 8, natural, 0)


EXT = pltpu.VMEM(((WIDE * TILE + 16) * SPAN, LANE), jnp.float32)
ACC = pltpu.VMEM((BINS + 1, SUB, LANE), jnp.float32)


def middle(kernel, name, table, count, own, lo, hi):
    return pl.pallas_call(
        kernel,
        out_shape=(FULL, EDGE, EDGE),
        in_specs=[SM, SM, VM, VM, VM],
        out_specs=(VM, VM, VM),
        scratch_shapes=[EXT, ACC],
        compiler_params=params(),
        name=name,
    )(table, count, own, lo, hi)


def last(table, count, own, lo, hi):
    return pl.pallas_call(
        third_kernel,
        out_shape=jax.ShapeDtypeStruct((TILE, TILE, SUB * LANE), jnp.float32),
        in_specs=[SM, SM, VM, VM, VM],
        out_specs=VM,
        scratch_shapes=[
            EXT,
            pltpu.VMEM(((BINS + 1) * SUB, LANE), jnp.float32),
            pltpu.VMEM((1024, LANE), jnp.float32),
        ],
        compiler_params=params(),
        name="third",
    )(table, count, own, lo, hi)


def beside(head, tail, axis):
    ends = lax.axis_size(axis) - 1
    lo = lax.ppermute(tail, axis, [(i, i + 1) for i in range(ends)])
    hi = lax.ppermute(head, axis, [(i + 1, i) for i in range(ends)])
    return lo, hi


def on_device(traces, destination, bin_index, dip_inline, dip_cross):
    x = traces.reshape(DEV, 4, 8, 128).transpose(0, 2, 1, 3).reshape(4096, 128)
    outgoing = pack(destination.reshape(-1), bin_index.reshape(-1), x)
    arrived = lax.all_to_all(
        outgoing, ("inline", "crosslin"), split_axis=0, concat_axis=0, tiled=True
    )
    dips = jnp.concatenate([dip_inline.reshape(-1), dip_cross.reshape(-1)])
    table, count = make_lists(dips)
    bins = arrived[:, 64, :8].astype(jnp.int32).reshape(-1)
    fold = jnp.sum(
        (jnp.arange(BINS, dtype=jnp.int32)[:, None] == bins[None, :]).astype(jnp.float32), axis=1
    )
    stacked, head, tail = put_bins(bins, 1.0 / jnp.maximum(fold, 1.0), arrived)
    lo, hi = beside(head, tail, "inline")
    first, left, right = middle(first_kernel, "first", table, count, stacked, lo, hi)
    lo, hi = beside(left, right, "crosslin")
    second, head, tail = middle(second_kernel, "second", table, count, first, lo, hi)
    lo, hi = beside(head, tail, "inline")
    return last(table, count, second, lo, hi)


def solution(mesh):
    return jax.shard_map(
        on_device,
        mesh=mesh,
        in_specs=(
            P(("inline", "crosslin"), None, None),
            P(("inline", "crosslin"), None),
            P(("inline", "crosslin"), None),
            P("inline", "crosslin"),
            P("inline", "crosslin"),
        ),
        out_specs=P("inline", "crosslin", None),
        check_vma=False,
    )
```

```python
import functools

import jax
import jax.numpy as jnp
from jax import lax
from jax.experimental import pallas as pl
from jax.experimental.pallas import tpu as pltpu
from jax.sharding import PartitionSpec as P

HALF = 7
DMAX = 2
DIPS = 2 * DMAX + 1
TILE = 32
BINS = TILE * TILE
DEV = 128
SUB, LANE = 8, 128
SPAN = 40
GROUP = 8
ROOM = 18 * TILE + GROUP
PAY = 72
HALO = HALF * TILE

VM = pl.BlockSpec(memory_space=pltpu.VMEM)
SM = pl.BlockSpec(memory_space=pltpu.SMEM)
HB = pl.BlockSpec(memory_space=pl.ANY)


def params():
    return pltpu.CompilerParams(vmem_limit_bytes=60 << 20)


def pack_kernel(dest, bins, x, out, scr, z, brow, cnt, sem, bsem):
    for tr in range(4):
        for j in range(8):
            z[pl.ds(j * 128, 128), :] = x[pl.ds(j * 4 + tr, 128, stride=32), :].T
        for ti in range(SUB):
            scr[pl.ds(tr * 8 + ti, 128, stride=32), :] = z[pl.ds(ti, 128, stride=8), :].T
    brow[...] = jnp.full((DEV, 1, LANE), float(BINS), jnp.float32)

    def clear(i, _):
        cnt[i] = 0
        return 0

    lax.fori_loop(0, DEV, clear, 0, unroll=8)
    lane = lax.broadcasted_iota(jnp.int32, (1, LANE), 1)

    def place(b, _):
        t = dest[b]
        rank = cnt[t]
        cnt[t] = rank + 1
        pltpu.make_async_copy(
            scr.at[pl.ds(b * 32, 32)], out.at[t, pl.ds(rank * 32, 32)], sem
        ).start()
        row = brow[t]
        for q in range(4):
            row = jnp.where(lane == rank * 4 + q, bins[b * 4 + q].astype(jnp.float32), row)
        brow[t] = row
        return 0

    lax.fori_loop(0, DEV, place, 0)
    copy = pltpu.make_async_copy(brow, out.at[:, pl.ds(64, 1)], bsem)
    copy.start()
    pltpu.make_async_copy(scr, scr, sem).wait()
    copy.wait()


def pack(dest, bins, x):
    return pl.pallas_call(
        pack_kernel,
        out_shape=jax.ShapeDtypeStruct((DEV, PAY, LANE), jnp.float32),
        in_specs=[SM, SM, VM],
        out_specs=HB,
        scratch_shapes=[
            pltpu.VMEM((4096, LANE), jnp.float32),
            pltpu.VMEM((1024, LANE), jnp.float32),
            pltpu.VMEM((DEV, 1, LANE), jnp.float32),
            pltpu.SMEM((DEV,), jnp.int32),
            pltpu.SemaphoreType.DMA,
            pltpu.SemaphoreType.DMA,
        ],
        compiler_params=params(),
        name="pack",
    )(dest, bins, x)


def add_bin(dips, table, count, i, part):
    at = part * DIPS + dips[i] + DMAX
    n = count[at]
    table[at * ROOM + n] = i
    count[at] = n + 1


def lists_kernel(along_rows, dips, table, count):
    for at in range(2 * DIPS):
        count[at] = 0
    inside = range(HALF, TILE - HALF)
    if along_rows:
        for low, high, part in ((0, HALF, 1), (HALF, TILE - HALF, 0), (TILE - HALF, TILE, 1)):

            def add(i, _):
                add_bin(dips, table, count, i, part)
                return 0

            lax.fori_loop(low * TILE, high * TILE, add, 0, unroll=4)
    else:

        def row(r, _):
            for c in range(TILE):
                add_bin(dips, table, count, r * TILE + c, 0 if c in inside else 1)
            return 0

        lax.fori_loop(0, TILE, row, 0)
    for at in range(2 * DIPS):
        n = count[at]
        for u in range(GROUP):
            table[at * ROOM + n + u] = BINS


def make_lists(dips, along_rows):
    return pl.pallas_call(
        functools.partial(lists_kernel, along_rows),
        out_shape=(
            jax.ShapeDtypeStruct((2 * DIPS * ROOM,), jnp.int32),
            jax.ShapeDtypeStruct((2 * DIPS,), jnp.int32),
        ),
        in_specs=[SM],
        out_specs=(SM, SM),
        compiler_params=params(),
        cost_estimate=pl.CostEstimate(flops=0, bytes_accessed=24 << 20, transcendentals=0),
        name="lists_rows" if along_rows else "lists_cols",
    )(dips)


def bin_kernel(bins, scale, x, out, head, tail, *sums):
    zero = jnp.zeros((SUB, LANE), jnp.float32)

    def clear(i, _):
        for s in sums:
            s[i] = zero
        return 0

    lax.fori_loop(0, BINS, clear, 0, unroll=8)

    def add(i, _):
        for slot in range(2):
            for tr in range(4):
                b = bins[i * 8 + slot * 4 + tr]
                sums[tr][b] += x[i, pl.ds(slot * 32 + tr * 8, 8), :]
        return 0

    lax.fori_loop(0, DEV, add, 0, unroll=2)

    def finish(i, _):
        out[i] = ((sums[0][i] + sums[1][i]) + (sums[2][i] + sums[3][i])) * scale[i]
        return 0

    lax.fori_loop(0, BINS, finish, 0, unroll=8)
    head[...] = out[pl.ds(0, HALO)]
    tail[...] = out[pl.ds(BINS - HALO, HALO)]


FULL = jax.ShapeDtypeStruct((BINS, SUB, LANE), jnp.float32)
EDGE = jax.ShapeDtypeStruct((HALO, SUB, LANE), jnp.float32)


def put_bins(bins, scale, x):
    return pl.pallas_call(
        bin_kernel,
        out_shape=(FULL, EDGE, EDGE),
        in_specs=[SM, SM, VM],
        out_specs=(VM, VM, VM),
        scratch_shapes=[pltpu.VMEM((BINS + 1, SUB, LANE), jnp.float32) for _ in range(4)],
        compiler_params=params(),
        name="put_bins",
    )(bins, scale, x)


def widen(ext, row, x, lane):
    ext[pl.ds(row + 16, 8), :] = x
    ext[pl.ds(row + 24, 8), :] = jnp.where(lane < 127, pltpu.roll(x, 127, 1), 0.0)
    ext[pl.ds(row + 32, 8), :] = jnp.where(lane < 126, pltpu.roll(x, 126, 1), 0.0)
    ext[pl.ds(row + 8, 8), :] = jnp.where(lane >= 1, pltpu.roll(x, 1, 1), 0.0)
    ext[pl.ds(row, 8), :] = jnp.where(lane >= 2, pltpu.roll(x, 2, 1), 0.0)


WIDE = TILE + 2 * HALF
ROW_PITCH = TILE * SPAN + 8
COL_PITCH = SPAN
EXT_ROWS = 72000


def start_of(b, along_rows):
    if along_rows:
        return b * SPAN + 8 * (b >> 5)
    return (b + 2 * HALF * (b >> 5)) * SPAN


def inner_margins(ext, own, along_rows):
    lane = lax.broadcasted_iota(jnp.int32, (SUB, LANE), 1)
    shift = HALF * (ROW_PITCH if along_rows else COL_PITCH)

    def row(r, _):
        first = start_of(r * TILE, along_rows) + shift

        def inner(c, _):
            widen(ext, pl.multiple_of(first + c * SPAN, 8), own[r * TILE + c], lane)
            return 0

        lax.fori_loop(0, TILE, inner, 0, unroll=16)
        return 0

    lax.fori_loop(0, TILE, row, 0)


def outer_margins(ext, lo, hi, along_rows):
    lane = lax.broadcasted_iota(jnp.int32, (SUB, LANE), 1)
    if along_rows:

        def row(r, _):
            first = r * ROW_PITCH

            def outer(c, _):
                at = pl.multiple_of(first + c * SPAN, 8)
                widen(ext, at, lo[r * TILE + c], lane)
                widen(
                    ext,
                    pl.multiple_of(at + (TILE + HALF) * ROW_PITCH, 8),
                    hi[r * TILE + c],
                    lane,
                )
                return 0

            lax.fori_loop(0, TILE, outer, 0, unroll=8)
            return 0

        lax.fori_loop(0, HALF, row, 0)
    else:

        def row(r, _):
            first = pl.multiple_of(r * WIDE * SPAN, 8)
            for c in range(HALF):
                widen(ext, first + c * SPAN, lo[r * HALF + c], lane)
                widen(ext, first + (HALF + TILE + c) * SPAN, hi[r * HALF + c], lane)
            return 0

        lax.fori_loop(0, TILE, row, 0)


def steer(table, count, part, ext, along_rows, acc):
    pitch = ROW_PITCH if along_rows else COL_PITCH
    for d in range(-DMAX, DMAX + 1):
        at = part * DIPS + d + DMAX

        def group(g, _):
            for u in range(GROUP):
                b = table[at * ROOM + g * GROUP + u]
                first = pl.multiple_of(start_of(b, along_rows), 8)
                view = ext.at[pl.ds(first, 14 * pitch + SPAN)]

                def tap(k):
                    return view[pl.ds(16 + (k + HALF) * pitch + d * k, 8), :]

                total = tap(0) * (1.0 / 8.0)
                for k in range(1, HALF + 1):
                    total = total + (tap(k) + tap(-k)) * ((HALF + 1 - k) / 64.0)
                acc[b] = total
            return 0

        lax.fori_loop(0, (count[at] + GROUP - 1) // GROUP, group, 0)


def inner_kernel(along_rows, table, count, own, ext, acc):
    inner_margins(ext, own, along_rows)
    steer(table, count, 0, ext, along_rows, acc)


def outer_kernel(along_rows, table, count, lo, hi, ext_in, acc_in, ext, acc, one, two):
    outer_margins(ext, lo, hi, along_rows)
    steer(table, count, 1, ext, along_rows, acc)
    if along_rows:

        def cut(r, _):
            for c in range(HALF):
                one[r * HALF + c] = acc[r * TILE + c]
                two[r * HALF + c] = acc[r * TILE + TILE - HALF + c]
            return 0

        lax.fori_loop(0, TILE, cut, 0)
    else:
        one[...] = acc[pl.ds(0, HALO)]
        two[...] = acc[pl.ds(BINS - HALO, HALO)]


def natural(acc, out, z, i):
    for ti in range(SUB):
        z[pl.ds(ti, 128, stride=8), :] = acc[pl.ds(i * 128, 128), ti, :].T
    for j in range(8):
        out[pl.ds(i * 4, 4), :, pl.ds(j * 128, 128)] = (
            z[pl.ds(j * 128, 128), :].T.reshape(4, 32, 128)
        )


def last_kernel(table, count, lo, hi, ext_in, acc_in, out, ext, acc, z):
    outer_margins(ext, lo, hi, True)
    steer(table, count, 1, ext, True, acc)

    def four(i, _):
        natural(acc, out, z, i)
        return 0

    lax.fori_loop(0, 8, four, 0)


EXT = pltpu.VMEM((EXT_ROWS, LANE), jnp.float32)
ACC = pltpu.VMEM((BINS + 1, SUB, LANE), jnp.float32)


def small():
    return pltpu.CompilerParams(vmem_limit_bytes=16 << 20)


def inner(lists, own, along_rows):
    return pl.pallas_call(
        functools.partial(inner_kernel, along_rows),
        out_shape=(EXT, ACC),
        in_specs=[SM, SM, VM],
        out_specs=(VM, VM),
        compiler_params=small(),
        cost_estimate=pl.CostEstimate(flops=0, bytes_accessed=48 << 20, transcendentals=0),
        name="inner_rows" if along_rows else "inner_cols",
    )(*lists, own)


def outer(lists, lo, hi, kept, along_rows):
    return pl.pallas_call(
        functools.partial(outer_kernel, along_rows),
        out_shape=(EXT, ACC, EDGE, EDGE),
        in_specs=[SM, SM, VM, VM, VM, VM],
        out_specs=(VM, VM, VM, VM),
        input_output_aliases={4: 0, 5: 1},
        compiler_params=small(),
        name="outer_rows" if along_rows else "outer_cols",
    )(*lists, lo, hi, *kept)[1:]


def last(lists, lo, hi, kept):
    return pl.pallas_call(
        last_kernel,
        out_shape=(jax.ShapeDtypeStruct((TILE, TILE, SUB * LANE), jnp.float32), EXT, ACC),
        in_specs=[SM, SM, VM, VM, VM, VM],
        out_specs=(VM, VM, VM),
        input_output_aliases={4: 1, 5: 2},
        scratch_shapes=[pltpu.VMEM((1024, LANE), jnp.float32)],
        compiler_params=small(),
        name="last",
    )(*lists, lo, hi, *kept)[0]


def beside(head, tail, axis):
    ends = lax.axis_size(axis) - 1
    lo = lax.ppermute(tail, axis, [(i, i + 1) for i in range(ends)])
    hi = lax.ppermute(head, axis, [(i + 1, i) for i in range(ends)])
    return lo, hi


def on_device(traces, destination, bin_index, dip_inline, dip_cross):
    x = traces.reshape(DEV, 4, 8, 128).transpose(0, 2, 1, 3).reshape(4096, 128)
    outgoing = pack(destination.reshape(-1), bin_index.reshape(-1), x)
    arrived = lax.all_to_all(
        outgoing, ("inline", "crosslin"), split_axis=0, concat_axis=0, tiled=True
    )
    rows = make_lists(dip_inline.reshape(-1), True)
    cols = make_lists(dip_cross.reshape(-1), False)
    bins = arrived[:, 64, :8].astype(jnp.int32).reshape(-1)
    fold = jnp.sum(
        (jnp.arange(BINS, dtype=jnp.int32)[:, None] == bins[None, :]).astype(jnp.float32), axis=1
    )
    stacked, head, tail = put_bins(bins, 1.0 / jnp.maximum(fold, 1.0), arrived)
    lo, hi = beside(head, tail, "inline")
    kept = inner(rows, stacked, True)
    first, left, right = outer(rows, lo, hi, kept, True)
    lo, hi = beside(left, right, "crosslin")
    kept = inner(cols, first, False)
    second, head, tail = outer(cols, lo, hi, kept, False)
    lo, hi = beside(head, tail, "inline")
    kept = inner(rows, second, True)
    return last(rows, lo, hi, kept)


def solution(mesh):
    return jax.shard_map(
        on_device,
        mesh=mesh,
        in_specs=(
            P(("inline", "crosslin"), None, None),
            P(("inline", "crosslin"), None),
            P(("inline", "crosslin"), None),
            P("inline", "crosslin"),
            P("inline", "crosslin"),
        ),
        out_specs=P("inline", "crosslin", None),
        check_vma=False,
    )
```

```python
import functools

import jax
import jax.numpy as jnp
from jax import lax
from jax.experimental import pallas as pl
from jax.experimental.pallas import tpu as pltpu
from jax.sharding import PartitionSpec as P

HALF = 7
DMAX = 2
DIPS = 2 * DMAX + 1
TILE = 32
BINS = TILE * TILE
DEV = 128
SUB, LANE = 8, 128
SPAN = 40
GROUP = 16
MORE = 4
ROOM = 18 * TILE + GROUP
PAY = 72
HALO = HALF * TILE

VM = pl.BlockSpec(memory_space=pltpu.VMEM)
SM = pl.BlockSpec(memory_space=pltpu.SMEM)
HB = pl.BlockSpec(memory_space=pl.ANY)


def params():
    return pltpu.CompilerParams(vmem_limit_bytes=60 << 20)


def pack_kernel(dest, bins, x, out, scr, z, brow, cnt, sem, bsem):
    for tr in range(4):
        for j in range(8):
            z[pl.ds(j * 128, 128), :] = x[pl.ds(j * 4 + tr, 128, stride=32), :].T
        for ti in range(SUB):
            scr[pl.ds(tr * 8 + ti, 128, stride=32), :] = z[pl.ds(ti, 128, stride=8), :].T
    brow[...] = jnp.full((DEV, 1, LANE), float(BINS), jnp.float32)

    def clear(i, _):
        cnt[i] = 0
        return 0

    lax.fori_loop(0, DEV, clear, 0, unroll=8)
    lane = lax.broadcasted_iota(jnp.int32, (1, LANE), 1)

    def place(b, _):
        t = dest[b]
        rank = cnt[t]
        cnt[t] = rank + 1
        pltpu.make_async_copy(
            scr.at[pl.ds(b * 32, 32)], out.at[t, pl.ds(rank * 32, 32)], sem
        ).start()
        row = brow[t]
        for q in range(4):
            row = jnp.where(lane == rank * 4 + q, bins[b * 4 + q].astype(jnp.float32), row)
        brow[t] = row
        return 0

    lax.fori_loop(0, DEV, place, 0)
    copy = pltpu.make_async_copy(brow, out.at[:, pl.ds(64, 1)], bsem)
    copy.start()
    pltpu.make_async_copy(scr, scr, sem).wait()
    copy.wait()


def pack(dest, bins, x):
    return pl.pallas_call(
        pack_kernel,
        out_shape=jax.ShapeDtypeStruct((DEV, PAY, LANE), jnp.float32),
        in_specs=[SM, SM, VM],
        out_specs=HB,
        scratch_shapes=[
            pltpu.VMEM((4096, LANE), jnp.float32),
            pltpu.VMEM((1024, LANE), jnp.float32),
            pltpu.VMEM((DEV, 1, LANE), jnp.float32),
            pltpu.SMEM((DEV,), jnp.int32),
            pltpu.SemaphoreType.DMA,
            pltpu.SemaphoreType.DMA,
        ],
        compiler_params=params(),
        name="pack",
    )(dest, bins, x)


def add_bin(dips, table, count, i, part):
    at = part * DIPS + dips[i] + DMAX
    n = count[at]
    table[at * ROOM + n] = i
    count[at] = n + 1


def lists_kernel(along_rows, dips, table, count):
    for at in range(2 * DIPS):
        count[at] = 0
    inside = range(HALF, TILE - HALF)
    if along_rows:
        for low, high, part in ((0, HALF, 1), (HALF, TILE - HALF, 0), (TILE - HALF, TILE, 1)):

            def add(i, _):
                add_bin(dips, table, count, i, part)
                return 0

            lax.fori_loop(low * TILE, high * TILE, add, 0, unroll=4)
    else:

        def row(r, _):
            for c in range(TILE):
                add_bin(dips, table, count, r * TILE + c, 0 if c in inside else 1)
            return 0

        lax.fori_loop(0, TILE, row, 0)
    for at in range(2 * DIPS):
        n = count[at]
        for u in range(GROUP):
            table[at * ROOM + n + u] = BINS


def both_lists_kernel(dip_rows, dip_cols, table_rows, count_rows, table_cols, count_cols):
    lists_kernel(True, dip_rows, table_rows, count_rows)
    lists_kernel(False, dip_cols, table_cols, count_cols)


def make_lists(dip_rows, dip_cols):
    table = jax.ShapeDtypeStruct((2 * DIPS * ROOM,), jnp.int32)
    count = jax.ShapeDtypeStruct((2 * DIPS,), jnp.int32)
    table_rows, count_rows, table_cols, count_cols = pl.pallas_call(
        both_lists_kernel,
        out_shape=(table, count, table, count),
        in_specs=[SM, SM],
        out_specs=(SM,) * 4,
        compiler_params=params(),
        cost_estimate=pl.CostEstimate(flops=0, bytes_accessed=24 << 20, transcendentals=0),
        name="lists",
    )(dip_rows, dip_cols)
    return (table_rows, count_rows), (table_cols, count_cols)


def bin_kernel(bins, scale, x_hbm, out, head, tail, x, sems, *sums):
    chunk = DEV // MORE
    copies = [
        pltpu.make_async_copy(
            x_hbm.at[pl.ds(q * chunk, chunk), pl.ds(0, 64)], x.at[pl.ds(q * chunk, chunk)], sems.at[q]
        )
        for q in range(MORE)
    ]
    for copy in copies:
        copy.start()
    zero = jnp.zeros((SUB, LANE), jnp.float32)

    def clear(i, _):
        for s in sums:
            s[i] = zero
        return 0

    lax.fori_loop(0, BINS, clear, 0, unroll=8)

    def add(i, _):
        for slot in range(2):
            for tr in range(4):
                b = bins[i * 8 + slot * 4 + tr]
                sums[tr][b] += x[i, pl.ds(slot * 32 + tr * 8, 8), :]
        return 0

    for q in range(MORE):
        copies[q].wait()
        lax.fori_loop(q * chunk, (q + 1) * chunk, add, 0, unroll=2)

    def finish(i, _):
        out[i] = ((sums[0][i] + sums[1][i]) + (sums[2][i] + sums[3][i])) * scale[i]
        return 0

    lax.fori_loop(0, BINS, finish, 0, unroll=8)
    head[...] = out[pl.ds(0, HALO)]
    tail[...] = out[pl.ds(BINS - HALO, HALO)]


FULL = jax.ShapeDtypeStruct((BINS, SUB, LANE), jnp.float32)
EDGE = jax.ShapeDtypeStruct((HALO, SUB, LANE), jnp.float32)


def put_bins(bins, scale, x):
    return pl.pallas_call(
        bin_kernel,
        out_shape=(FULL, EDGE, EDGE),
        in_specs=[SM, SM, HB],
        out_specs=(VM, VM, VM),
        scratch_shapes=[
            pltpu.VMEM((DEV, 64, LANE), jnp.float32),
            pltpu.SemaphoreType.DMA((MORE,)),
            *[pltpu.VMEM((BINS + 1, SUB, LANE), jnp.float32) for _ in range(4)],
        ],
        compiler_params=params(),
        name="put_bins",
    )(bins, scale, x)


def shift_matrix():
    k = lax.broadcasted_iota(jnp.int32, (2 * LANE, 4 * LANE), 0) % LANE
    n = lax.broadcasted_iota(jnp.int32, (2 * LANE, 4 * LANE), 1)
    block = n // LANE
    move = jnp.where(block < 2, block - 2, block - 1)
    return jnp.where(k == n % LANE + move, 1.0, 0.0).astype(jnp.bfloat16)


def widen(ext, starts, x, mat):
    n = x.shape[0]
    flat = x.reshape(n * SUB, LANE)
    high = flat.astype(jnp.bfloat16)
    low = (flat - high.astype(jnp.float32)).astype(jnp.bfloat16)
    moved = jnp.dot(
        jnp.concatenate([high, low], axis=1), mat[...], preferred_element_type=jnp.float32
    )
    for u in range(n):
        at = starts[u]
        ext[pl.ds(at + 16, 8), :] = flat[u * 8 : u * 8 + 8]
        for block, offset in enumerate((0, 8, 24, 32)):
            ext[pl.ds(at + offset, 8), :] = moved[
                u * 8 : u * 8 + 8, block * LANE : (block + 1) * LANE
            ]


WIDE = TILE + 2 * HALF
ROW_PITCH = TILE * SPAN + 8
COL_PITCH = SPAN
EXT_ROWS = 72000


def start_of(b, along_rows):
    if along_rows:
        return b * SPAN + 8 * (b >> 5)
    return (b + 2 * HALF * (b >> 5)) * SPAN


def inner_margins(ext, own_hbm, own, sems, mat, along_rows):
    mat[...] = shift_matrix()
    shift = HALF * (ROW_PITCH if along_rows else COL_PITCH)
    chunk = BINS // MORE
    copies = [
        pltpu.make_async_copy(
            own_hbm.at[pl.ds(q * chunk, chunk)], own.at[pl.ds(q * chunk, chunk)], sems.at[q]
        )
        for q in range(MORE)
    ]
    for copy in copies:
        copy.start()

    def row(r, _):
        first = start_of(r * TILE, along_rows) + shift
        starts = [pl.multiple_of(first + c * SPAN, 8) for c in range(TILE)]
        widen(ext, starts, own[pl.ds(r * TILE, TILE)], mat)
        return 0

    for q in range(MORE):
        copies[q].wait()
        lax.fori_loop(q * TILE // MORE, (q + 1) * TILE // MORE, row, 0)


def outer_margins(ext, lo_hbm, hi_hbm, lo, hi, sems, mat, along_rows):
    copies = [
        pltpu.make_async_copy(lo_hbm, lo, sems.at[0]),
        pltpu.make_async_copy(hi_hbm, hi, sems.at[1]),
    ]
    for copy in copies:
        copy.start()
    mat[...] = shift_matrix()
    for side, ref in enumerate((lo, hi)):
        copies[side].wait()
        beyond = side * (TILE + HALF)
        if along_rows:

            def row(r, _):
                first = (r + beyond) * ROW_PITCH
                starts = [pl.multiple_of(first + c * SPAN, 8) for c in range(TILE)]
                widen(ext, starts, ref[pl.ds(r * TILE, TILE)], mat)
                return 0

            lax.fori_loop(0, HALF, row, 0)
        else:

            def four_rows(q, _):
                starts = [
                    pl.multiple_of(((q * 4 + p) * WIDE + beyond + c) * SPAN, 8)
                    for p in range(4)
                    for c in range(HALF)
                ]
                widen(ext, starts, ref[pl.ds(q * 4 * HALF, 4 * HALF)], mat)
                return 0

            lax.fori_loop(0, TILE // 4, four_rows, 0)


def steer(table, count, part, ext, along_rows, acc):
    pitch = ROW_PITCH if along_rows else COL_PITCH
    for d in range(-DMAX, DMAX + 1):
        at = part * DIPS + d + DMAX

        def group(g, _):
            for u in range(GROUP):
                b = table[at * ROOM + g * GROUP + u]
                first = pl.multiple_of(start_of(b, along_rows), 8)
                view = ext.at[pl.ds(first, 14 * pitch + SPAN)]

                def tap(k):
                    return view[pl.ds(16 + (k + HALF) * pitch + d * k, 8), :]

                total = tap(0) * (1.0 / 8.0)
                for k in range(1, HALF + 1):
                    total = total + (tap(k) + tap(-k)) * ((HALF + 1 - k) / 64.0)
                acc[b] = total
            return 0

        lax.fori_loop(0, (count[at] + GROUP - 1) // GROUP, group, 0)


def inner_kernel(along_rows, table, count, own_hbm, ext, acc, own, sems, mat):
    inner_margins(ext, own_hbm, own, sems, mat, along_rows)
    steer(table, count, 0, ext, along_rows, acc)


def outer_kernel(
    along_rows, table, count, lo_hbm, hi_hbm, ext_in, acc_in, ext, acc, one, two, lo, hi, sems, mat
):
    outer_margins(ext, lo_hbm, hi_hbm, lo, hi, sems, mat, along_rows)
    steer(table, count, 1, ext, along_rows, acc)
    if along_rows:

        def cut(r, _):
            for c in range(HALF):
                one[r * HALF + c] = acc[r * TILE + c]
                two[r * HALF + c] = acc[r * TILE + TILE - HALF + c]
            return 0

        lax.fori_loop(0, TILE, cut, 0)
    else:
        one[...] = acc[pl.ds(0, HALO)]
        two[...] = acc[pl.ds(BINS - HALO, HALO)]


def natural(acc, out_hbm, z, parts, sems, groups):
    copies = []
    for slot, i in enumerate(groups):
        for ti in range(SUB):
            z[pl.ds(ti, 128, stride=8), :] = acc[pl.ds(i * 128, 128), ti, :].T
        for j in range(8):
            parts[slot, :, :, pl.ds(j * 128, 128)] = (
                z[pl.ds(j * 128, 128), :].T.reshape(4, TILE, 128)
            )
        copy = pltpu.make_async_copy(parts.at[slot], out_hbm.at[pl.ds(i * 4, 4)], sems.at[slot])
        copy.start()
        copies.append(copy)
    for copy in copies:
        copy.wait()


def inner_last_kernel(table, count, own_hbm, ext, acc, out_hbm, own, sems, mat, z, parts, outs):
    inner_kernel(True, table, count, own_hbm, ext, acc, own, sems, mat)
    natural(acc, out_hbm, z, parts, outs, (2, 3, 4, 5))


def last_kernel(
    table, count, lo_hbm, hi_hbm, ext_in, acc_in, out_in, ext, acc, out_hbm,
    lo, hi, sems, mat, z, parts, outs,
):
    outer_margins(ext, lo_hbm, hi_hbm, lo, hi, sems, mat, True)
    steer(table, count, 1, ext, True, acc)
    natural(acc, out_hbm, z, parts, outs, (0, 1, 6, 7))


EXT = pltpu.VMEM((EXT_ROWS, LANE), jnp.float32)
ACC = pltpu.VMEM((BINS + 1, SUB, LANE), jnp.float32)


def small():
    return pltpu.CompilerParams(vmem_limit_bytes=16 << 20)


OWN = [
    pltpu.VMEM((BINS, SUB, LANE), jnp.float32),
    pltpu.SemaphoreType.DMA((MORE,)),
    pltpu.VMEM((2 * LANE, 4 * LANE), jnp.bfloat16),
]
SIDES = [
    pltpu.VMEM((HALO, SUB, LANE), jnp.float32),
    pltpu.VMEM((HALO, SUB, LANE), jnp.float32),
    pltpu.SemaphoreType.DMA((2,)),
    pltpu.VMEM((2 * LANE, 4 * LANE), jnp.bfloat16),
]
PARTS = [
    pltpu.VMEM((1024, LANE), jnp.float32),
    pltpu.VMEM((4, 4, TILE, SUB * LANE), jnp.float32),
    pltpu.SemaphoreType.DMA((4,)),
]
RESULT = jax.ShapeDtypeStruct((TILE, TILE, SUB * LANE), jnp.float32)
BUSY = pl.CostEstimate(flops=0, bytes_accessed=48 << 20, transcendentals=0)


def inner(lists, own, along_rows):
    return pl.pallas_call(
        functools.partial(inner_kernel, along_rows),
        out_shape=(EXT, ACC),
        in_specs=[SM, SM, HB],
        out_specs=(VM, VM),
        scratch_shapes=OWN,
        compiler_params=small(),
        cost_estimate=BUSY,
        name="inner_rows" if along_rows else "inner_cols",
    )(*lists, own)


def outer(lists, lo, hi, kept, along_rows):
    return pl.pallas_call(
        functools.partial(outer_kernel, along_rows),
        out_shape=(EXT, ACC, EDGE, EDGE),
        in_specs=[SM, SM, HB, HB, VM, VM],
        out_specs=(VM, VM, VM, VM),
        scratch_shapes=SIDES,
        input_output_aliases={4: 0, 5: 1},
        compiler_params=small(),
        name="outer_rows" if along_rows else "outer_cols",
    )(*lists, lo, hi, *kept)[1:]


def inner_last(lists, own):
    return pl.pallas_call(
        inner_last_kernel,
        out_shape=(EXT, ACC, RESULT),
        in_specs=[SM, SM, HB],
        out_specs=(VM, VM, HB),
        scratch_shapes=OWN + PARTS,
        compiler_params=small(),
        cost_estimate=BUSY,
        name="inner_last",
    )(*lists, own)


def last(lists, lo, hi, kept):
    return pl.pallas_call(
        last_kernel,
        out_shape=(EXT, ACC, RESULT),
        in_specs=[SM, SM, HB, HB, VM, VM, HB],
        out_specs=(VM, VM, HB),
        scratch_shapes=SIDES + PARTS,
        input_output_aliases={4: 0, 5: 1, 6: 2},
        compiler_params=small(),
        name="last",
    )(*lists, lo, hi, *kept)[2]


def beside(head, tail, axis):
    ends = lax.axis_size(axis) - 1
    lo = lax.ppermute(tail, axis, [(i, i + 1) for i in range(ends)])
    hi = lax.ppermute(head, axis, [(i + 1, i) for i in range(ends)])
    return lo, hi


def on_device(traces, destination, bin_index, dip_inline, dip_cross):
    x = traces.reshape(DEV, 4, 8, 128).transpose(0, 2, 1, 3).reshape(4096, 128)
    outgoing = pack(destination.reshape(-1), bin_index.reshape(-1), x)
    arrived = lax.all_to_all(
        outgoing, ("inline", "crosslin"), split_axis=0, concat_axis=0, tiled=True
    )
    rows, cols = make_lists(dip_inline.reshape(-1), dip_cross.reshape(-1))
    bins = arrived[:, 64, :8].astype(jnp.int32).reshape(-1)
    fold = jnp.sum(
        (jnp.arange(BINS, dtype=jnp.int32)[:, None] == bins[None, :]).astype(jnp.float32), axis=1
    )
    stacked, head, tail = put_bins(bins, 1.0 / jnp.maximum(fold, 1.0), arrived)
    lo, hi = beside(head, tail, "inline")
    kept = inner(rows, stacked, True)
    first, left, right = outer(rows, lo, hi, kept, True)
    lo, hi = beside(left, right, "crosslin")
    kept = inner(cols, first, False)
    second, head, tail = outer(cols, lo, hi, kept, False)
    lo, hi = beside(head, tail, "inline")
    kept = inner_last(rows, second)
    return last(rows, lo, hi, kept)


def solution(mesh):
    return jax.shard_map(
        on_device,
        mesh=mesh,
        in_specs=(
            P(("inline", "crosslin"), None, None),
            P(("inline", "crosslin"), None),
            P(("inline", "crosslin"), None),
            P("inline", "crosslin"),
            P("inline", "crosslin"),
        ),
        out_specs=P("inline", "crosslin", None),
        check_vma=False,
    )
```

```python
import functools

import jax
import jax.numpy as jnp
from jax import lax
from jax.experimental import pallas as pl
from jax.experimental.pallas import tpu as pltpu
from jax.sharding import PartitionSpec as P

HALF = 7
DMAX = 2
DIPS = 2 * DMAX + 1
TILE = 32
BINS = TILE * TILE
DEV = 128
SUB, LANE = 8, 128
SPAN = 40
GROUP = 16
MORE = 4
ROOM = 18 * TILE + GROUP
PAY = 72
HALO = HALF * TILE

VM = pl.BlockSpec(memory_space=pltpu.VMEM)
SM = pl.BlockSpec(memory_space=pltpu.SMEM)
HB = pl.BlockSpec(memory_space=pl.ANY)


def params():
    return pltpu.CompilerParams(vmem_limit_bytes=60 << 20)


def pack_kernel(dest, bins, x, out, scr, z, brow, cnt, sem, bsem):
    for tr in range(4):
        for j in range(8):
            z[pl.ds(j * 128, 128), :] = x[pl.ds(j * 4 + tr, 128, stride=32), :].T
        for ti in range(SUB):
            scr[pl.ds(tr * 8 + ti, 128, stride=32), :] = z[pl.ds(ti, 128, stride=8), :].T
    brow[...] = jnp.full((DEV, 1, LANE), float(BINS), jnp.float32)

    def clear(i, _):
        cnt[i] = 0
        return 0

    lax.fori_loop(0, DEV, clear, 0, unroll=8)
    lane = lax.broadcasted_iota(jnp.int32, (1, LANE), 1)

    def place(b, _):
        t = dest[b]
        rank = cnt[t]
        cnt[t] = rank + 1
        pltpu.make_async_copy(
            scr.at[pl.ds(b * 32, 32)], out.at[t, pl.ds(rank * 32, 32)], sem
        ).start()
        row = brow[t]
        for q in range(4):
            row = jnp.where(lane == rank * 4 + q, bins[b * 4 + q].astype(jnp.float32), row)
        brow[t] = row
        return 0

    lax.fori_loop(0, DEV, place, 0)
    copy = pltpu.make_async_copy(brow, out.at[:, pl.ds(64, 1)], bsem)
    copy.start()
    pltpu.make_async_copy(scr, scr, sem).wait()
    copy.wait()


def pack(dest, bins, x):
    return pl.pallas_call(
        pack_kernel,
        out_shape=jax.ShapeDtypeStruct((DEV, PAY, LANE), jnp.float32),
        in_specs=[SM, SM, VM],
        out_specs=HB,
        scratch_shapes=[
            pltpu.VMEM((4096, LANE), jnp.float32),
            pltpu.VMEM((1024, LANE), jnp.float32),
            pltpu.VMEM((DEV, 1, LANE), jnp.float32),
            pltpu.SMEM((DEV,), jnp.int32),
            pltpu.SemaphoreType.DMA,
            pltpu.SemaphoreType.DMA,
        ],
        compiler_params=params(),
        name="pack",
    )(dest, bins, x)


USED = 65


def exchange_kernel(x, out, send, recv, near):
    inline, crosslin = lax.axis_size("inline"), lax.axis_size("crosslin")
    i, j = lax.axis_index("inline"), lax.axis_index("crosslin")
    me = i * crosslin + j

    def peer(s):
        return lax.rem(i + s // crosslin, inline), lax.rem(j + lax.rem(s, crosslin), crosslin)

    barrier = pltpu.get_barrier_semaphore()

    def greet(s, _):
        pl.semaphore_signal(
            barrier, inc=1, device_id=peer(s), device_id_type=pl.DeviceIdType.MESH
        )
        return 0

    lax.fori_loop(1, DEV, greet, 0)
    stay = pltpu.make_async_copy(x.at[me, pl.ds(0, USED)], out.at[me, pl.ds(0, USED)], near)
    stay.start()
    pl.semaphore_wait(barrier, DEV - 1)

    def post(s, _):
        pi, pj = peer(s)
        pltpu.make_async_remote_copy(
            src_ref=x.at[pi * crosslin + pj, pl.ds(0, USED)],
            dst_ref=out.at[me, pl.ds(0, USED)],
            send_sem=send,
            recv_sem=recv,
            device_id=(pi, pj),
            device_id_type=pl.DeviceIdType.MESH,
        ).start()
        return 0

    lax.fori_loop(1, DEV, post, 0)
    stay.wait()
    rest = x.at[pl.ds(0, DEV - 1), pl.ds(0, USED)]
    pltpu.make_async_copy(rest, rest, send).wait()
    pltpu.make_async_copy(rest, rest, recv).wait()


def exchange(x):
    return pl.pallas_call(
        exchange_kernel,
        out_shape=jax.ShapeDtypeStruct((DEV, PAY, LANE), jnp.float32),
        in_specs=[HB],
        out_specs=HB,
        scratch_shapes=[pltpu.SemaphoreType.DMA] * 3,
        compiler_params=pltpu.CompilerParams(
            collective_id=0, has_side_effects=True, vmem_limit_bytes=62 << 20
        ),
        name="exchange",
    )(x)


def add_bin(dips, table, count, i, part):
    at = part * DIPS + dips[i] + DMAX
    n = count[at]
    table[at * ROOM + n] = i
    count[at] = n + 1


def lists_kernel(along_rows, dips, table, count):
    for at in range(2 * DIPS):
        count[at] = 0
    inside = range(HALF, TILE - HALF)
    if along_rows:
        for low, high, part in ((0, HALF, 1), (HALF, TILE - HALF, 0), (TILE - HALF, TILE, 1)):

            def add(i, _):
                add_bin(dips, table, count, i, part)
                return 0

            lax.fori_loop(low * TILE, high * TILE, add, 0, unroll=4)
    else:

        def row(r, _):
            for c in range(TILE):
                add_bin(dips, table, count, r * TILE + c, 0 if c in inside else 1)
            return 0

        lax.fori_loop(0, TILE, row, 0)
    for at in range(2 * DIPS):
        n = count[at]
        for u in range(GROUP):
            table[at * ROOM + n + u] = BINS


def both_lists_kernel(dip_rows, dip_cols, table_rows, count_rows, table_cols, count_cols):
    lists_kernel(True, dip_rows, table_rows, count_rows)
    lists_kernel(False, dip_cols, table_cols, count_cols)


def make_lists(dip_rows, dip_cols):
    table = jax.ShapeDtypeStruct((2 * DIPS * ROOM,), jnp.int32)
    count = jax.ShapeDtypeStruct((2 * DIPS,), jnp.int32)
    table_rows, count_rows, table_cols, count_cols = pl.pallas_call(
        both_lists_kernel,
        out_shape=(table, count, table, count),
        in_specs=[SM, SM],
        out_specs=(SM,) * 4,
        compiler_params=params(),
        cost_estimate=pl.CostEstimate(flops=0, bytes_accessed=24 << 20, transcendentals=0),
        name="lists",
    )(dip_rows, dip_cols)
    return (table_rows, count_rows), (table_cols, count_cols)


def bin_kernel(bins, scale, x_hbm, out, head, tail, x, sems, *sums):
    chunk = DEV // MORE
    copies = [
        pltpu.make_async_copy(
            x_hbm.at[pl.ds(q * chunk, chunk), pl.ds(0, 64)], x.at[pl.ds(q * chunk, chunk)], sems.at[q]
        )
        for q in range(MORE)
    ]
    for copy in copies:
        copy.start()
    zero = jnp.zeros((SUB, LANE), jnp.float32)

    def clear(i, _):
        for s in sums:
            s[i] = zero
        return 0

    lax.fori_loop(0, BINS, clear, 0, unroll=8)

    def add(i, _):
        for slot in range(2):
            for tr in range(4):
                b = bins[i * 8 + slot * 4 + tr]
                sums[tr][b] += x[i, pl.ds(slot * 32 + tr * 8, 8), :]
        return 0

    for q in range(MORE):
        copies[q].wait()
        lax.fori_loop(q * chunk, (q + 1) * chunk, add, 0, unroll=2)

    def finish(i, _):
        out[i] = ((sums[0][i] + sums[1][i]) + (sums[2][i] + sums[3][i])) * scale[i]
        return 0

    lax.fori_loop(0, BINS, finish, 0, unroll=8)
    head[...] = out[pl.ds(0, HALO)]
    tail[...] = out[pl.ds(BINS - HALO, HALO)]


FULL = jax.ShapeDtypeStruct((BINS, SUB, LANE), jnp.float32)
EDGE = jax.ShapeDtypeStruct((HALO, SUB, LANE), jnp.float32)


def put_bins(bins, scale, x):
    return pl.pallas_call(
        bin_kernel,
        out_shape=(FULL, EDGE, EDGE),
        in_specs=[SM, SM, HB],
        out_specs=(VM, VM, VM),
        scratch_shapes=[
            pltpu.VMEM((DEV, 64, LANE), jnp.float32),
            pltpu.SemaphoreType.DMA((MORE,)),
            *[pltpu.VMEM((BINS + 1, SUB, LANE), jnp.float32) for _ in range(4)],
        ],
        compiler_params=params(),
        name="put_bins",
    )(bins, scale, x)


def shift_matrix():
    k = lax.broadcasted_iota(jnp.int32, (2 * LANE, 4 * LANE), 0) % LANE
    n = lax.broadcasted_iota(jnp.int32, (2 * LANE, 4 * LANE), 1)
    block = n // LANE
    move = jnp.where(block < 2, block - 2, block - 1)
    return jnp.where(k == n % LANE + move, 1.0, 0.0).astype(jnp.bfloat16)


def widen(ext, starts, x, mat):
    n = x.shape[0]
    flat = x.reshape(n * SUB, LANE)
    high = flat.astype(jnp.bfloat16)
    low = (flat - high.astype(jnp.float32)).astype(jnp.bfloat16)
    moved = jnp.dot(
        jnp.concatenate([high, low], axis=1), mat[...], preferred_element_type=jnp.float32
    )
    for u in range(n):
        at = starts[u]
        ext[pl.ds(at + 16, 8), :] = flat[u * 8 : u * 8 + 8]
        for block, offset in enumerate((0, 8, 24, 32)):
            ext[pl.ds(at + offset, 8), :] = moved[
                u * 8 : u * 8 + 8, block * LANE : (block + 1) * LANE
            ]


WIDE = TILE + 2 * HALF
ROW_PITCH = TILE * SPAN + 8
COL_PITCH = SPAN
EXT_ROWS = 72000


def start_of(b, along_rows):
    if along_rows:
        return b * SPAN + 8 * (b >> 5)
    return (b + 2 * HALF * (b >> 5)) * SPAN


def inner_margins(ext, own_hbm, own, sems, mat, along_rows):
    mat[...] = shift_matrix()
    shift = HALF * (ROW_PITCH if along_rows else COL_PITCH)
    chunk = BINS // MORE
    copies = [
        pltpu.make_async_copy(
            own_hbm.at[pl.ds(q * chunk, chunk)], own.at[pl.ds(q * chunk, chunk)], sems.at[q]
        )
        for q in range(MORE)
    ]
    for copy in copies:
        copy.start()

    def row(r, _):
        first = start_of(r * TILE, along_rows) + shift
        starts = [pl.multiple_of(first + c * SPAN, 8) for c in range(TILE)]
        widen(ext, starts, own[pl.ds(r * TILE, TILE)], mat)
        return 0

    for q in range(MORE):
        copies[q].wait()
        lax.fori_loop(q * TILE // MORE, (q + 1) * TILE // MORE, row, 0)


def outer_margins(ext, lo_hbm, hi_hbm, lo, hi, sems, mat, along_rows):
    copies = [
        pltpu.make_async_copy(lo_hbm, lo, sems.at[0]),
        pltpu.make_async_copy(hi_hbm, hi, sems.at[1]),
    ]
    for copy in copies:
        copy.start()
    mat[...] = shift_matrix()
    for side, ref in enumerate((lo, hi)):
        copies[side].wait()
        beyond = side * (TILE + HALF)
        if along_rows:

            def row(r, _):
                first = (r + beyond) * ROW_PITCH
                starts = [pl.multiple_of(first + c * SPAN, 8) for c in range(TILE)]
                widen(ext, starts, ref[pl.ds(r * TILE, TILE)], mat)
                return 0

            lax.fori_loop(0, HALF, row, 0)
        else:

            def four_rows(q, _):
                starts = [
                    pl.multiple_of(((q * 4 + p) * WIDE + beyond + c) * SPAN, 8)
                    for p in range(4)
                    for c in range(HALF)
                ]
                widen(ext, starts, ref[pl.ds(q * 4 * HALF, 4 * HALF)], mat)
                return 0

            lax.fori_loop(0, TILE // 4, four_rows, 0)


def steer(table, count, part, ext, along_rows, acc):
    pitch = ROW_PITCH if along_rows else COL_PITCH
    for d in range(-DMAX, DMAX + 1):
        at = part * DIPS + d + DMAX

        def group(g, _):
            for u in range(GROUP):
                b = table[at * ROOM + g * GROUP + u]
                first = pl.multiple_of(start_of(b, along_rows), 8)
                view = ext.at[pl.ds(first, 14 * pitch + SPAN)]

                def tap(k):
                    return view[pl.ds(16 + (k + HALF) * pitch + d * k, 8), :]

                total = tap(0) * (1.0 / 8.0)
                for k in range(1, HALF + 1):
                    total = total + (tap(k) + tap(-k)) * ((HALF + 1 - k) / 64.0)
                acc[b] = total
            return 0

        lax.fori_loop(0, (count[at] + GROUP - 1) // GROUP, group, 0)


def inner_kernel(along_rows, table, count, own_hbm, ext, acc, own, sems, mat):
    inner_margins(ext, own_hbm, own, sems, mat, along_rows)
    steer(table, count, 0, ext, along_rows, acc)


def outer_kernel(
    along_rows, table, count, lo_hbm, hi_hbm, ext_in, acc_in, ext, acc, one, two, lo, hi, sems, mat
):
    outer_margins(ext, lo_hbm, hi_hbm, lo, hi, sems, mat, along_rows)
    steer(table, count, 1, ext, along_rows, acc)
    if along_rows:

        def cut(r, _):
            for c in range(HALF):
                one[r * HALF + c] = acc[r * TILE + c]
                two[r * HALF + c] = acc[r * TILE + TILE - HALF + c]
            return 0

        lax.fori_loop(0, TILE, cut, 0)
    else:
        one[...] = acc[pl.ds(0, HALO)]
        two[...] = acc[pl.ds(BINS - HALO, HALO)]


def natural(acc, out_hbm, z, parts, sems, groups):
    copies = []
    for slot, i in enumerate(groups):
        for ti in range(SUB):
            z[pl.ds(ti, 128, stride=8), :] = acc[pl.ds(i * 128, 128), ti, :].T
        for j in range(8):
            parts[slot, :, :, pl.ds(j * 128, 128)] = (
                z[pl.ds(j * 128, 128), :].T.reshape(4, TILE, 128)
            )
        copy = pltpu.make_async_copy(parts.at[slot], out_hbm.at[pl.ds(i * 4, 4)], sems.at[slot])
        copy.start()
        copies.append(copy)
    for copy in copies:
        copy.wait()


def inner_last_kernel(table, count, own_hbm, ext, acc, out_hbm, own, sems, mat, z, parts, outs):
    inner_kernel(True, table, count, own_hbm, ext, acc, own, sems, mat)
    natural(acc, out_hbm, z, parts, outs, (2, 3, 4, 5))


def last_kernel(
    table, count, lo_hbm, hi_hbm, ext_in, acc_in, out_in, ext, acc, out_hbm,
    lo, hi, sems, mat, z, parts, outs,
):
    outer_margins(ext, lo_hbm, hi_hbm, lo, hi, sems, mat, True)
    steer(table, count, 1, ext, True, acc)
    natural(acc, out_hbm, z, parts, outs, (0, 1, 6, 7))


EXT = pltpu.VMEM((EXT_ROWS, LANE), jnp.float32)
ACC = pltpu.VMEM((BINS + 1, SUB, LANE), jnp.float32)


def small(mib):
    return pltpu.CompilerParams(vmem_limit_bytes=mib << 20)


OWN = [
    pltpu.VMEM((BINS, SUB, LANE), jnp.float32),
    pltpu.SemaphoreType.DMA((MORE,)),
    pltpu.VMEM((2 * LANE, 4 * LANE), jnp.bfloat16),
]
SIDES = [
    pltpu.VMEM((HALO, SUB, LANE), jnp.float32),
    pltpu.VMEM((HALO, SUB, LANE), jnp.float32),
    pltpu.SemaphoreType.DMA((2,)),
    pltpu.VMEM((2 * LANE, 4 * LANE), jnp.bfloat16),
]
PARTS = [
    pltpu.VMEM((1024, LANE), jnp.float32),
    pltpu.VMEM((4, 4, TILE, SUB * LANE), jnp.float32),
    pltpu.SemaphoreType.DMA((4,)),
]
RESULT = jax.ShapeDtypeStruct((TILE, TILE, SUB * LANE), jnp.float32)
BUSY = pl.CostEstimate(flops=0, bytes_accessed=48 << 20, transcendentals=0)


def inner(lists, own, along_rows):
    return pl.pallas_call(
        functools.partial(inner_kernel, along_rows),
        out_shape=(EXT, ACC),
        in_specs=[SM, SM, HB],
        out_specs=(VM, VM),
        scratch_shapes=OWN,
        compiler_params=small(12),
        cost_estimate=BUSY,
        name="inner_rows" if along_rows else "inner_cols",
    )(*lists, own)


def outer(lists, lo, hi, kept, along_rows):
    return pl.pallas_call(
        functools.partial(outer_kernel, along_rows),
        out_shape=(EXT, ACC, EDGE, EDGE),
        in_specs=[SM, SM, HB, HB, VM, VM],
        out_specs=(VM, VM, VM, VM),
        scratch_shapes=SIDES,
        input_output_aliases={4: 0, 5: 1},
        compiler_params=small(12),
        name="outer_rows" if along_rows else "outer_cols",
    )(*lists, lo, hi, *kept)[1:]


def inner_last(lists, own):
    return pl.pallas_call(
        inner_last_kernel,
        out_shape=(EXT, ACC, RESULT),
        in_specs=[SM, SM, HB],
        out_specs=(VM, VM, HB),
        scratch_shapes=OWN + PARTS,
        compiler_params=small(12),
        cost_estimate=BUSY,
        name="inner_last",
    )(*lists, own)


def last(lists, lo, hi, kept):
    return pl.pallas_call(
        last_kernel,
        out_shape=(EXT, ACC, RESULT),
        in_specs=[SM, SM, HB, HB, VM, VM, HB],
        out_specs=(VM, VM, HB),
        scratch_shapes=SIDES + PARTS,
        input_output_aliases={4: 0, 5: 1, 6: 2},
        compiler_params=small(12),
        name="last",
    )(*lists, lo, hi, *kept)[2]


def beside(head, tail, axis):
    ends = lax.axis_size(axis) - 1
    lo = lax.ppermute(tail, axis, [(i, i + 1) for i in range(ends)])
    hi = lax.ppermute(head, axis, [(i + 1, i) for i in range(ends)])
    return lo, hi


def on_device(traces, destination, bin_index, dip_inline, dip_cross):
    x = traces.reshape(DEV, 4, 8, 128).transpose(0, 2, 1, 3).reshape(4096, 128)
    outgoing = pack(destination.reshape(-1), bin_index.reshape(-1), x)
    arrived = exchange(outgoing)
    rows, cols = make_lists(dip_inline.reshape(-1), dip_cross.reshape(-1))
    bins = arrived[:, 64, :8].astype(jnp.int32).reshape(-1)
    fold = jnp.sum(
        (jnp.arange(BINS, dtype=jnp.int32)[:, None] == bins[None, :]).astype(jnp.float32), axis=1
    )
    stacked, head, tail = put_bins(bins, 1.0 / jnp.maximum(fold, 1.0), arrived)
    lo, hi = beside(head, tail, "inline")
    kept = inner(rows, stacked, True)
    first, left, right = outer(rows, lo, hi, kept, True)
    lo, hi = beside(left, right, "crosslin")
    kept = inner(cols, first, False)
    second, head, tail = outer(cols, lo, hi, kept, False)
    lo, hi = beside(head, tail, "inline")
    kept = inner_last(rows, second)
    return last(rows, lo, hi, kept)


def solution(mesh):
    return jax.shard_map(
        on_device,
        mesh=mesh,
        in_specs=(
            P(("inline", "crosslin"), None, None),
            P(("inline", "crosslin"), None),
            P(("inline", "crosslin"), None),
            P("inline", "crosslin"),
            P("inline", "crosslin"),
        ),
        out_specs=P("inline", "crosslin", None),
        check_vma=False,
    )
```

```python
import functools

import jax
import jax.numpy as jnp
from jax import lax
from jax.experimental import pallas as pl
from jax.experimental.pallas import tpu as pltpu
from jax.sharding import PartitionSpec as P

HALF = 7
DMAX = 2
DIPS = 2 * DMAX + 1
TILE = 32
BINS = TILE * TILE
DEV = 128
SUB, LANE = 8, 128
SPAN = 40
GROUP = 16
MORE = 4
ROOM = 18 * TILE + GROUP
PAY = 65
HALO = HALF * TILE

VM = pl.BlockSpec(memory_space=pltpu.VMEM)
SM = pl.BlockSpec(memory_space=pltpu.SMEM)
HB = pl.BlockSpec(memory_space=pl.ANY)


def params():
    return pltpu.CompilerParams(vmem_limit_bytes=60 << 20)


def pack_kernel(dest, bins, x, out, scr, z, brow, cnt, sem, bsem):
    for tr in range(4):
        for j in range(8):
            z[pl.ds(j * 128, 128), :] = x[pl.ds(j * 4 + tr, 128, stride=32), :].T
        for ti in range(SUB):
            scr[pl.ds(tr * 8 + ti, 128, stride=32), :] = z[pl.ds(ti, 128, stride=8), :].T
    brow[...] = jnp.full((DEV, 1, LANE), float(BINS), jnp.float32)

    def clear(i, _):
        cnt[i] = 0
        return 0

    lax.fori_loop(0, DEV, clear, 0, unroll=8)
    lane = lax.broadcasted_iota(jnp.int32, (1, LANE), 1)

    def place(b, _):
        t = dest[b]
        rank = cnt[t]
        cnt[t] = rank + 1
        pltpu.make_async_copy(
            scr.at[pl.ds(b * 32, 32)], out.at[t, pl.ds(rank * 32, 32), 0], sem
        ).start()
        row = brow[t]
        for q in range(4):
            row = jnp.where(lane == rank * 4 + q, bins[q, b].astype(jnp.float32), row)
        brow[t] = row
        return 0

    lax.fori_loop(0, DEV, place, 0)
    copy = pltpu.make_async_copy(brow, out.at[:, 64], bsem)
    copy.start()
    pltpu.make_async_copy(scr, scr, sem).wait()
    copy.wait()


def pack(dest, bins, x):
    return pl.pallas_call(
        pack_kernel,
        out_shape=jax.ShapeDtypeStruct((DEV, PAY, 1, LANE), jnp.float32),
        in_specs=[SM, SM, VM],
        out_specs=HB,
        scratch_shapes=[
            pltpu.VMEM((4096, LANE), jnp.float32),
            pltpu.VMEM((1024, LANE), jnp.float32),
            pltpu.VMEM((DEV, 1, LANE), jnp.float32),
            pltpu.SMEM((DEV,), jnp.int32),
            pltpu.SemaphoreType.DMA,
            pltpu.SemaphoreType.DMA,
        ],
        compiler_params=params(),
        name="pack",
    )(dest, bins, x)


def add_bin(dips, table, count, i, part):
    at = part * DIPS + dips[i] + DMAX
    n = count[at]
    table[at * ROOM + n] = i
    count[at] = n + 1


def lists_kernel(along_rows, dips, table, count):
    for at in range(2 * DIPS):
        count[at] = 0
    inside = range(HALF, TILE - HALF)
    if along_rows:
        for low, high, part in ((0, HALF, 1), (HALF, TILE - HALF, 0), (TILE - HALF, TILE, 1)):

            def add(i, _):
                add_bin(dips, table, count, i, part)
                return 0

            lax.fori_loop(low * TILE, high * TILE, add, 0, unroll=4)
    else:

        def row(r, _):
            for c in range(TILE):
                add_bin(dips, table, count, r * TILE + c, 0 if c in inside else 1)
            return 0

        lax.fori_loop(0, TILE, row, 0)
    for at in range(2 * DIPS):
        n = count[at]
        for u in range(GROUP):
            table[at * ROOM + n + u] = BINS


def both_lists_kernel(dip_rows, dip_cols, table_rows, count_rows, table_cols, count_cols):
    lists_kernel(True, dip_rows, table_rows, count_rows)
    lists_kernel(False, dip_cols, table_cols, count_cols)


def make_lists(dip_rows, dip_cols):
    table = jax.ShapeDtypeStruct((2 * DIPS * ROOM,), jnp.int32)
    count = jax.ShapeDtypeStruct((2 * DIPS,), jnp.int32)
    table_rows, count_rows, table_cols, count_cols = pl.pallas_call(
        both_lists_kernel,
        out_shape=(table, count, table, count),
        in_specs=[SM, SM],
        out_specs=(SM,) * 4,
        compiler_params=params(),
        cost_estimate=pl.CostEstimate(flops=0, bytes_accessed=24 << 20, transcendentals=0),
        name="lists",
    )(dip_rows, dip_cols)
    return (table_rows, count_rows), (table_cols, count_cols)


def bin_kernel(bins, scale, x_hbm, out, head, tail, x, sems, *sums):
    chunk = DEV // MORE
    copies = [
        pltpu.make_async_copy(
            x_hbm.at[pl.ds(q * chunk, chunk), pl.ds(0, 64), 0], x.at[pl.ds(q * chunk, chunk)], sems.at[q]
        )
        for q in range(MORE)
    ]
    for copy in copies:
        copy.start()
    zero = jnp.zeros((SUB, LANE), jnp.float32)

    def clear(i, _):
        for s in sums:
            s[i] = zero
        return 0

    lax.fori_loop(0, BINS, clear, 0, unroll=8)

    def add(i, _):
        for slot in range(2):
            for tr in range(4):
                b = bins[i * 8 + slot * 4 + tr]
                sums[tr][b] += x[i, pl.ds(slot * 32 + tr * 8, 8), :]
        return 0

    for q in range(MORE):
        copies[q].wait()
        lax.fori_loop(q * chunk, (q + 1) * chunk, add, 0, unroll=2)

    def finish(i, _):
        out[i] = ((sums[0][i] + sums[1][i]) + (sums[2][i] + sums[3][i])) * scale[i]
        return 0

    lax.fori_loop(0, BINS, finish, 0, unroll=8)
    head[...] = out[pl.ds(0, HALO)]
    tail[...] = out[pl.ds(BINS - HALO, HALO)]


FULL = jax.ShapeDtypeStruct((BINS, SUB, LANE), jnp.float32)
EDGE = jax.ShapeDtypeStruct((HALO, SUB, LANE), jnp.float32)


def put_bins(bins, scale, x):
    return pl.pallas_call(
        bin_kernel,
        out_shape=(FULL, EDGE, EDGE),
        in_specs=[SM, SM, HB],
        out_specs=(VM, VM, VM),
        scratch_shapes=[
            pltpu.VMEM((DEV, 64, LANE), jnp.float32),
            pltpu.SemaphoreType.DMA((MORE,)),
            *[pltpu.VMEM((BINS + 1, SUB, LANE), jnp.float32) for _ in range(4)],
        ],
        compiler_params=small(58),
        name="put_bins",
    )(bins, scale, x)


def shift_matrix():
    k = lax.broadcasted_iota(jnp.int32, (2 * LANE, 4 * LANE), 0) % LANE
    n = lax.broadcasted_iota(jnp.int32, (2 * LANE, 4 * LANE), 1)
    block = n // LANE
    move = jnp.where(block < 2, block - 2, block - 1)
    return jnp.where(k == n % LANE + move, 1.0, 0.0).astype(jnp.bfloat16)


def widen(ext, starts, x, mat):
    n = x.shape[0]
    flat = x.reshape(n * SUB, LANE)
    high = flat.astype(jnp.bfloat16)
    low = (flat - high.astype(jnp.float32)).astype(jnp.bfloat16)
    moved = jnp.dot(
        jnp.concatenate([high, low], axis=1), mat[...], preferred_element_type=jnp.float32
    )
    for u in range(n):
        at = starts[u]
        ext[pl.ds(at + 16, 8), :] = flat[u * 8 : u * 8 + 8]
        for block, offset in enumerate((0, 8, 24, 32)):
            ext[pl.ds(at + offset, 8), :] = moved[
                u * 8 : u * 8 + 8, block * LANE : (block + 1) * LANE
            ]


WIDE = TILE + 2 * HALF
ROW_PITCH = TILE * SPAN + 8
COL_PITCH = SPAN
EXT_ROWS = 72000


def start_of(b, along_rows):
    if along_rows:
        return b * SPAN + 8 * (b >> 5)
    return (b + 2 * HALF * (b >> 5)) * SPAN


def inner_margins(ext, own_hbm, own, sems, mat, along_rows):
    mat[...] = shift_matrix()
    shift = HALF * (ROW_PITCH if along_rows else COL_PITCH)
    chunk = BINS // MORE
    copies = [
        pltpu.make_async_copy(
            own_hbm.at[pl.ds(q * chunk, chunk)], own.at[pl.ds(q * chunk, chunk)], sems.at[q]
        )
        for q in range(MORE)
    ]
    for copy in copies:
        copy.start()

    def row(r, _):
        first = start_of(r * TILE, along_rows) + shift
        starts = [pl.multiple_of(first + c * SPAN, 8) for c in range(TILE)]
        widen(ext, starts, own[pl.ds(r * TILE, TILE)], mat)
        return 0

    for q in range(MORE):
        copies[q].wait()
        lax.fori_loop(q * TILE // MORE, (q + 1) * TILE // MORE, row, 0)


def outer_margins(ext, lo_hbm, hi_hbm, lo, hi, sems, mat, along_rows):
    copies = [
        pltpu.make_async_copy(lo_hbm, lo, sems.at[0]),
        pltpu.make_async_copy(hi_hbm, hi, sems.at[1]),
    ]
    for copy in copies:
        copy.start()
    mat[...] = shift_matrix()
    for side, ref in enumerate((lo, hi)):
        copies[side].wait()
        beyond = side * (TILE + HALF)
        if along_rows:

            def row(r, _):
                first = (r + beyond) * ROW_PITCH
                starts = [pl.multiple_of(first + c * SPAN, 8) for c in range(TILE)]
                widen(ext, starts, ref[pl.ds(r * TILE, TILE)], mat)
                return 0

            lax.fori_loop(0, HALF, row, 0)
        else:

            def four_rows(q, _):
                starts = [
                    pl.multiple_of(((q * 4 + p) * WIDE + beyond + c) * SPAN, 8)
                    for p in range(4)
                    for c in range(HALF)
                ]
                widen(ext, starts, ref[pl.ds(q * 4 * HALF, 4 * HALF)], mat)
                return 0

            lax.fori_loop(0, TILE // 4, four_rows, 0)


def steer(table, count, part, ext, along_rows, acc):
    pitch = ROW_PITCH if along_rows else COL_PITCH
    for d in range(-DMAX, DMAX + 1):
        at = part * DIPS + d + DMAX

        def group(g, _):
            for u in range(GROUP):
                b = table[at * ROOM + g * GROUP + u]
                first = pl.multiple_of(start_of(b, along_rows), 8)
                view = ext.at[pl.ds(first, 14 * pitch + SPAN)]

                def tap(k):
                    return view[pl.ds(16 + (k + HALF) * pitch + d * k, 8), :]

                total = tap(0) * (1.0 / 8.0)
                for k in range(1, HALF + 1):
                    total = total + (tap(k) + tap(-k)) * ((HALF + 1 - k) / 64.0)
                acc[b] = total
            return 0

        lax.fori_loop(0, (count[at] + GROUP - 1) // GROUP, group, 0)


def inner_kernel(along_rows, table, count, own_hbm, ext, acc, own, sems, mat):
    inner_margins(ext, own_hbm, own, sems, mat, along_rows)
    steer(table, count, 0, ext, along_rows, acc)


def outer_kernel(
    along_rows, table, count, lo_hbm, hi_hbm, ext_in, acc_in,
    ext, acc, one, two, whole, lo, hi, sems, mat, away,
):
    outer_margins(ext, lo_hbm, hi_hbm, lo, hi, sems, mat, along_rows)
    steer(table, count, 1, ext, along_rows, acc)
    keep = pltpu.make_async_copy(acc.at[pl.ds(0, BINS)], whole, away)
    keep.start()
    if along_rows:

        def cut(r, _):
            for c in range(HALF):
                one[r * HALF + c] = acc[r * TILE + c]
                two[r * HALF + c] = acc[r * TILE + TILE - HALF + c]
            return 0

        lax.fori_loop(0, TILE, cut, 0)
    else:
        one[...] = acc[pl.ds(0, HALO)]
        two[...] = acc[pl.ds(BINS - HALO, HALO)]
    keep.wait()


def natural(acc, out_hbm, z, parts, sems, groups):
    copies = []
    for slot, i in enumerate(groups):
        for ti in range(SUB):
            z[pl.ds(ti, 128, stride=8), :] = acc[pl.ds(i * 128, 128), ti, :].T
        for j in range(8):
            parts[slot, :, :, pl.ds(j * 128, 128)] = (
                z[pl.ds(j * 128, 128), :].T.reshape(4, TILE, 128)
            )
        copy = pltpu.make_async_copy(parts.at[slot], out_hbm.at[pl.ds(i * 4, 4)], sems.at[slot])
        copy.start()
        copies.append(copy)
    for copy in copies:
        copy.wait()


def inner_last_kernel(table, count, own_hbm, ext, acc, out_hbm, own, sems, mat, z, parts, outs):
    inner_kernel(True, table, count, own_hbm, ext, acc, own, sems, mat)
    natural(acc, out_hbm, z, parts, outs, (2, 3, 4, 5))


def last_kernel(
    table, count, lo_hbm, hi_hbm, ext_in, acc_in, out_in, ext, acc, out_hbm,
    lo, hi, sems, mat, z, parts, outs,
):
    outer_margins(ext, lo_hbm, hi_hbm, lo, hi, sems, mat, True)
    steer(table, count, 1, ext, True, acc)
    natural(acc, out_hbm, z, parts, outs, (0, 1, 6, 7))


EXT = pltpu.VMEM((EXT_ROWS, LANE), jnp.float32)
ACC = pltpu.VMEM((BINS + 1, SUB, LANE), jnp.float32)


def small(mib):
    return pltpu.CompilerParams(vmem_limit_bytes=mib << 20)


OWN = [
    pltpu.VMEM((BINS, SUB, LANE), jnp.float32),
    pltpu.SemaphoreType.DMA((MORE,)),
    pltpu.VMEM((2 * LANE, 4 * LANE), jnp.bfloat16),
]
SIDES = [
    pltpu.VMEM((HALO, SUB, LANE), jnp.float32),
    pltpu.VMEM((HALO, SUB, LANE), jnp.float32),
    pltpu.SemaphoreType.DMA((2,)),
    pltpu.VMEM((2 * LANE, 4 * LANE), jnp.bfloat16),
]
PARTS = [
    pltpu.VMEM((1024, LANE), jnp.float32),
    pltpu.VMEM((4, 4, TILE, SUB * LANE), jnp.float32),
    pltpu.SemaphoreType.DMA((4,)),
]
RESULT = jax.ShapeDtypeStruct((TILE, TILE, SUB * LANE), jnp.float32)
BUSY = pl.CostEstimate(flops=0, bytes_accessed=48 << 20, transcendentals=0)


def inner(lists, own, along_rows):
    return pl.pallas_call(
        functools.partial(inner_kernel, along_rows),
        out_shape=(EXT, ACC),
        in_specs=[SM, SM, HB],
        out_specs=(VM, VM),
        scratch_shapes=OWN,
        compiler_params=small(12),
        cost_estimate=BUSY,
        name="inner_rows" if along_rows else "inner_cols",
    )(*lists, own)


def outer(lists, lo, hi, kept, along_rows):
    _, _, one, two, whole = pl.pallas_call(
        functools.partial(outer_kernel, along_rows),
        out_shape=(EXT, ACC, EDGE, EDGE, FULL),
        in_specs=[SM, SM, HB, HB, VM, VM],
        out_specs=(VM, VM, VM, VM, HB),
        scratch_shapes=SIDES + [pltpu.SemaphoreType.DMA],
        input_output_aliases={4: 0, 5: 1},
        compiler_params=small(12),
        name="outer_rows" if along_rows else "outer_cols",
    )(*lists, lo, hi, *kept)
    return whole, one, two


def inner_last(lists, own):
    return pl.pallas_call(
        inner_last_kernel,
        out_shape=(EXT, ACC, RESULT),
        in_specs=[SM, SM, HB],
        out_specs=(VM, VM, HB),
        scratch_shapes=OWN + PARTS,
        compiler_params=small(12),
        cost_estimate=BUSY,
        name="inner_last",
    )(*lists, own)


def last(lists, lo, hi, kept):
    return pl.pallas_call(
        last_kernel,
        out_shape=(EXT, ACC, RESULT),
        in_specs=[SM, SM, HB, HB, VM, VM, HB],
        out_specs=(VM, VM, HB),
        scratch_shapes=SIDES + PARTS,
        input_output_aliases={4: 0, 5: 1, 6: 2},
        compiler_params=small(12),
        name="last",
    )(*lists, lo, hi, *kept)[2]


def beside(head, tail, axis):
    ends = lax.axis_size(axis) - 1
    lo = lax.ppermute(tail, axis, [(i, i + 1) for i in range(ends)])
    hi = lax.ppermute(head, axis, [(i + 1, i) for i in range(ends)])
    return lo, hi


def on_device(traces, destination, bin_index, dip_inline, dip_cross):
    x = traces.reshape(DEV, 4, 8, 128).transpose(0, 2, 1, 3).reshape(4096, 128)
    outgoing = pack(destination.reshape(-1), bin_index.T, x)
    arrived = lax.all_to_all(
        outgoing, ("inline", "crosslin"), split_axis=0, concat_axis=0, tiled=True
    )
    rows, cols = make_lists(dip_inline.reshape(-1), dip_cross.reshape(-1))
    bins = arrived[:, 64, 0, :8].astype(jnp.int32).reshape(-1)
    fold = jnp.sum(
        (jnp.arange(BINS, dtype=jnp.int32)[:, None] == bins[None, :]).astype(jnp.float32), axis=1
    )
    stacked, head, tail = put_bins(bins, 1.0 / jnp.maximum(fold, 1.0), arrived)
    lo, hi = beside(head, tail, "inline")
    kept = inner(rows, stacked, True)
    first, left, right = outer(rows, lo, hi, kept, True)
    lo, hi = beside(left, right, "crosslin")
    kept = inner(cols, first, False)
    second, head, tail = outer(cols, lo, hi, kept, False)
    lo, hi = beside(head, tail, "inline")
    kept = inner_last(rows, second)
    return last(rows, lo, hi, kept)


def solution(mesh):
    return jax.shard_map(
        on_device,
        mesh=mesh,
        in_specs=(
            P(("inline", "crosslin"), None, None),
            P(("inline", "crosslin"), None),
            P(("inline", "crosslin"), None),
            P("inline", "crosslin"),
            P("inline", "crosslin"),
        ),
        out_specs=P("inline", "crosslin", None),
        check_vma=False,
    )
```

```python
import functools

import jax
import jax.numpy as jnp
from jax import lax
from jax.experimental import pallas as pl
from jax.experimental.pallas import tpu as pltpu
from jax.sharding import PartitionSpec as P

HALF = 7
DMAX = 2
DIPS = 2 * DMAX + 1
TILE = 32
BINS = TILE * TILE
DEV = 128
SUB, LANE = 8, 128
SPAN = 40
GROUP = 16
MORE = 4
ROOM = 18 * TILE + GROUP
PAY = 65
HALO = HALF * TILE

VM = pl.BlockSpec(memory_space=pltpu.VMEM)
SM = pl.BlockSpec(memory_space=pltpu.SMEM)
HB = pl.BlockSpec(memory_space=pl.ANY)


def params():
    return pltpu.CompilerParams(vmem_limit_bytes=60 << 20)


def pack_kernel(dest, bins, x, out, scr, z, brow, cnt, sem, bsem):
    for tr in range(4):
        for j in range(8):
            z[pl.ds(j * 128, 128), :] = x[pl.ds(j * 4 + tr, 128, stride=32), :].T
        for ti in range(SUB):
            scr[pl.ds(tr * 8 + ti, 128, stride=32), :] = z[pl.ds(ti, 128, stride=8), :].T
    brow[...] = jnp.full((DEV, 1, LANE), float(BINS), jnp.float32)

    def clear(i, _):
        cnt[i] = 0
        return 0

    lax.fori_loop(0, DEV, clear, 0, unroll=8)
    lane = lax.broadcasted_iota(jnp.int32, (1, LANE), 1)

    def place(b, _):
        t = dest[b]
        rank = cnt[t]
        cnt[t] = rank + 1
        pltpu.make_async_copy(
            scr.at[pl.ds(b * 32, 32)], out.at[t, pl.ds(rank * 32, 32), 0], sem
        ).start()
        row = brow[t]
        for q in range(4):
            row = jnp.where(lane == rank * 4 + q, bins[q, b].astype(jnp.float32), row)
        brow[t] = row
        return 0

    lax.fori_loop(0, DEV, place, 0)
    copy = pltpu.make_async_copy(brow, out.at[:, 64], bsem)
    copy.start()
    pltpu.make_async_copy(scr, scr, sem).wait()
    copy.wait()


def pack(dest, bins, x):
    return pl.pallas_call(
        pack_kernel,
        out_shape=jax.ShapeDtypeStruct((DEV, PAY, 1, LANE), jnp.float32),
        in_specs=[SM, SM, VM],
        out_specs=HB,
        scratch_shapes=[
            pltpu.VMEM((4096, LANE), jnp.float32),
            pltpu.VMEM((1024, LANE), jnp.float32),
            pltpu.VMEM((DEV, 1, LANE), jnp.float32),
            pltpu.SMEM((DEV,), jnp.int32),
            pltpu.SemaphoreType.DMA,
            pltpu.SemaphoreType.DMA,
        ],
        compiler_params=params(),
        name="pack",
    )(dest, bins, x)


def add_bin(dips, table, count, i, part):
    at = dips[i] + (part * DIPS + DMAX)
    n = count[at]
    table[n] = i
    count[at] = n + 1


def lists_kernel(along_rows, dips, table, count):
    for at in range(2 * DIPS):
        count[at] = at * ROOM
    inside = range(HALF, TILE - HALF)
    if along_rows:
        for low, high, part in ((0, HALF, 1), (HALF, TILE - HALF, 0), (TILE - HALF, TILE, 1)):

            def add(i, _):
                add_bin(dips, table, count, i, part)
                return 0

            lax.fori_loop(low * TILE, high * TILE, add, 0, unroll=16)
    else:

        def row(r, _):
            for c in range(TILE):
                add_bin(dips, table, count, r * TILE + c, 0 if c in inside else 1)
            return 0

        lax.fori_loop(0, TILE, row, 0)
    for at in range(2 * DIPS):
        n = count[at]
        for u in range(GROUP):
            table[n + u] = BINS
        count[at] = n - at * ROOM


def both_lists_kernel(dip_rows, dip_cols, table_rows, count_rows, table_cols, count_cols):
    lists_kernel(True, dip_rows, table_rows, count_rows)
    lists_kernel(False, dip_cols, table_cols, count_cols)


def make_lists(dip_rows, dip_cols):
    table = jax.ShapeDtypeStruct((2 * DIPS * ROOM,), jnp.int32)
    count = jax.ShapeDtypeStruct((2 * DIPS,), jnp.int32)
    table_rows, count_rows, table_cols, count_cols = pl.pallas_call(
        both_lists_kernel,
        out_shape=(table, count, table, count),
        in_specs=[SM, SM],
        out_specs=(SM,) * 4,
        compiler_params=params(),
        cost_estimate=pl.CostEstimate(flops=0, bytes_accessed=24 << 20, transcendentals=0),
        name="lists",
    )(dip_rows, dip_cols)
    return (table_rows, count_rows), (table_cols, count_cols)


def bin_kernel(bins, scale, after, x_hbm, out, head, tail, x, sems, *sums):
    chunk = DEV // MORE
    copies = [
        pltpu.make_async_copy(
            x_hbm.at[pl.ds(q * chunk, chunk), pl.ds(0, 64), 0], x.at[pl.ds(q * chunk, chunk)], sems.at[q]
        )
        for q in range(MORE)
    ]
    for copy in copies:
        copy.start()
    zero = jnp.zeros((SUB, LANE), jnp.float32)

    def clear(i, _):
        for s in sums:
            s[i] = zero
        return 0

    lax.fori_loop(0, BINS, clear, 0, unroll=8)

    def add(i, _):
        for slot in range(2):
            for tr in range(4):
                b = bins[i * 8 + slot * 4 + tr]
                sums[tr][b] += x[i, pl.ds(slot * 32 + tr * 8, 8), :]
        return 0

    for q in range(MORE):
        copies[q].wait()
        lax.fori_loop(q * chunk, (q + 1) * chunk, add, 0, unroll=2)

    def finish(i, _):
        out[i] = ((sums[0][i] + sums[1][i]) + (sums[2][i] + sums[3][i])) * scale[i]
        return 0

    lax.fori_loop(0, BINS, finish, 0, unroll=8)
    head[...] = out[pl.ds(0, HALO)]
    tail[...] = out[pl.ds(BINS - HALO, HALO)]


FULL = jax.ShapeDtypeStruct((BINS, SUB, LANE), jnp.float32)
EDGE = jax.ShapeDtypeStruct((HALO, SUB, LANE), jnp.float32)


def put_bins(bins, scale, after, x):
    return pl.pallas_call(
        bin_kernel,
        out_shape=(FULL, EDGE, EDGE),
        in_specs=[SM, SM, SM, HB],
        out_specs=(VM, VM, VM),
        scratch_shapes=[
            pltpu.VMEM((DEV, 64, LANE), jnp.float32),
            pltpu.SemaphoreType.DMA((MORE,)),
            *[pltpu.VMEM((BINS + 1, SUB, LANE), jnp.float32) for _ in range(4)],
        ],
        compiler_params=small(58),
        name="put_bins",
    )(bins, scale, after, x)


def shift_matrix():
    k = lax.broadcasted_iota(jnp.int32, (2 * LANE, 4 * LANE), 0) % LANE
    n = lax.broadcasted_iota(jnp.int32, (2 * LANE, 4 * LANE), 1)
    block = n // LANE
    move = jnp.where(block < 2, block - 2, block - 1)
    return jnp.where(k == n % LANE + move, 1.0, 0.0).astype(jnp.bfloat16)


def widen(ext, starts, x, mat):
    n = x.shape[0]
    flat = x.reshape(n * SUB, LANE)
    high = flat.astype(jnp.bfloat16)
    low = (flat - high.astype(jnp.float32)).astype(jnp.bfloat16)
    moved = jnp.dot(
        jnp.concatenate([high, low], axis=1), mat[...], preferred_element_type=jnp.float32
    )
    for u in range(n):
        at = starts[u]
        ext[pl.ds(at + 16, 8), :] = flat[u * 8 : u * 8 + 8]
        for block, offset in enumerate((0, 8, 24, 32)):
            ext[pl.ds(at + offset, 8), :] = moved[
                u * 8 : u * 8 + 8, block * LANE : (block + 1) * LANE
            ]


WIDE = TILE + 2 * HALF
ROW_PITCH = TILE * SPAN + 8
COL_PITCH = SPAN
EXT_ROWS = 72000


def start_of(b, along_rows):
    if along_rows:
        return b * SPAN + 8 * (b >> 5)
    return (b + 2 * HALF * (b >> 5)) * SPAN


def inner_margins(ext, own_hbm, own, sems, mat, along_rows):
    mat[...] = shift_matrix()
    shift = HALF * (ROW_PITCH if along_rows else COL_PITCH)
    chunk = BINS // MORE
    copies = [
        pltpu.make_async_copy(
            own_hbm.at[pl.ds(q * chunk, chunk)], own.at[pl.ds(q * chunk, chunk)], sems.at[q]
        )
        for q in range(MORE)
    ]
    for copy in copies:
        copy.start()

    below = ROW_PITCH if along_rows else WIDE * SPAN

    def two_rows(r, _):
        first = start_of(r * 2 * TILE, along_rows) + shift
        starts = [
            pl.multiple_of(first + p * below + c * SPAN, 8) for p in range(2) for c in range(TILE)
        ]
        widen(ext, starts, own[pl.ds(r * 2 * TILE, 2 * TILE)], mat)
        return 0

    for q in range(MORE):
        copies[q].wait()
        lax.fori_loop(q * TILE // MORE // 2, (q + 1) * TILE // MORE // 2, two_rows, 0)


def outer_margins(ext, lo_hbm, hi_hbm, lo, hi, sems, mat, along_rows):
    copies = [
        pltpu.make_async_copy(lo_hbm, lo, sems.at[0]),
        pltpu.make_async_copy(hi_hbm, hi, sems.at[1]),
    ]
    for copy in copies:
        copy.start()
    mat[...] = shift_matrix()
    for side, ref in enumerate((lo, hi)):
        copies[side].wait()
        beyond = side * (TILE + HALF)
        if along_rows:

            def row(r, _):
                first = (r + beyond) * ROW_PITCH
                starts = [pl.multiple_of(first + c * SPAN, 8) for c in range(TILE)]
                widen(ext, starts, ref[pl.ds(r * TILE, TILE)], mat)
                return 0

            lax.fori_loop(0, HALF, row, 0)
        else:

            def four_rows(q, _):
                starts = [
                    pl.multiple_of(((q * 4 + p) * WIDE + beyond + c) * SPAN, 8)
                    for p in range(4)
                    for c in range(HALF)
                ]
                widen(ext, starts, ref[pl.ds(q * 4 * HALF, 4 * HALF)], mat)
                return 0

            lax.fori_loop(0, TILE // 4, four_rows, 0)


def steer(table, count, part, ext, along_rows, acc):
    pitch = ROW_PITCH if along_rows else COL_PITCH
    for d in range(-DMAX, DMAX + 1):
        at = part * DIPS + d + DMAX

        def group(g, _):
            for u in range(GROUP):
                b = table[at * ROOM + g * GROUP + u]
                first = pl.multiple_of(start_of(b, along_rows), 8)
                view = ext.at[pl.ds(first, 14 * pitch + SPAN)]

                def tap(k):
                    return view[pl.ds(16 + (k + HALF) * pitch + d * k, 8), :]

                total = tap(0) * (1.0 / 8.0)
                for k in range(1, HALF + 1):
                    total = total + (tap(k) + tap(-k)) * ((HALF + 1 - k) / 64.0)
                acc[b] = total
            return 0

        lax.fori_loop(0, (count[at] + GROUP - 1) // GROUP, group, 0)


def inner_kernel(along_rows, table, count, own_hbm, ext, acc, own, sems, mat):
    inner_margins(ext, own_hbm, own, sems, mat, along_rows)
    steer(table, count, 0, ext, along_rows, acc)


def outer_kernel(
    along_rows, table, count, lo_hbm, hi_hbm, ext_in, acc_in,
    ext, acc, one, two, whole, lo, hi, sems, mat, away,
):
    outer_margins(ext, lo_hbm, hi_hbm, lo, hi, sems, mat, along_rows)
    steer(table, count, 1, ext, along_rows, acc)
    keep = pltpu.make_async_copy(acc.at[pl.ds(0, BINS)], whole, away)
    keep.start()
    if along_rows:

        def cut(r, _):
            for c in range(HALF):
                one[r * HALF + c] = acc[r * TILE + c]
                two[r * HALF + c] = acc[r * TILE + TILE - HALF + c]
            return 0

        lax.fori_loop(0, TILE, cut, 0)
    else:
        one[...] = acc[pl.ds(0, HALO)]
        two[...] = acc[pl.ds(BINS - HALO, HALO)]
    keep.wait()


def natural(acc, out_hbm, z, parts, sems, groups):
    copies = []
    for slot, i in enumerate(groups):
        for ti in range(SUB):
            z[pl.ds(ti, 128, stride=8), :] = acc[pl.ds(i * 128, 128), ti, :].T
        for j in range(8):
            parts[slot, :, :, pl.ds(j * 128, 128)] = (
                z[pl.ds(j * 128, 128), :].T.reshape(4, TILE, 128)
            )
        copy = pltpu.make_async_copy(parts.at[slot], out_hbm.at[pl.ds(i * 4, 4)], sems.at[slot])
        copy.start()
        copies.append(copy)
    for copy in copies:
        copy.wait()


def inner_last_kernel(table, count, own_hbm, ext, acc, out_hbm, own, sems, mat, z, parts, outs):
    inner_kernel(True, table, count, own_hbm, ext, acc, own, sems, mat)
    natural(acc, out_hbm, z, parts, outs, (2, 3, 4, 5))


def last_kernel(
    table, count, lo_hbm, hi_hbm, ext_in, acc_in, out_in, ext, acc, out_hbm,
    lo, hi, sems, mat, z, parts, outs,
):
    outer_margins(ext, lo_hbm, hi_hbm, lo, hi, sems, mat, True)
    steer(table, count, 1, ext, True, acc)
    natural(acc, out_hbm, z, parts, outs, (0, 1, 6, 7))


EXT = pltpu.VMEM((EXT_ROWS, LANE), jnp.float32)
ACC = pltpu.VMEM((BINS + 1, SUB, LANE), jnp.float32)


def small(mib):
    return pltpu.CompilerParams(vmem_limit_bytes=mib << 20)


OWN = [
    pltpu.VMEM((BINS, SUB, LANE), jnp.float32),
    pltpu.SemaphoreType.DMA((MORE,)),
    pltpu.VMEM((2 * LANE, 4 * LANE), jnp.bfloat16),
]
SIDES = [
    pltpu.VMEM((HALO, SUB, LANE), jnp.float32),
    pltpu.VMEM((HALO, SUB, LANE), jnp.float32),
    pltpu.SemaphoreType.DMA((2,)),
    pltpu.VMEM((2 * LANE, 4 * LANE), jnp.bfloat16),
]
PARTS = [
    pltpu.VMEM((1024, LANE), jnp.float32),
    pltpu.VMEM((4, 4, TILE, SUB * LANE), jnp.float32),
    pltpu.SemaphoreType.DMA((4,)),
]
RESULT = jax.ShapeDtypeStruct((TILE, TILE, SUB * LANE), jnp.float32)
BUSY = pl.CostEstimate(flops=0, bytes_accessed=48 << 20, transcendentals=0)


def inner(lists, own, along_rows):
    return pl.pallas_call(
        functools.partial(inner_kernel, along_rows),
        out_shape=(EXT, ACC),
        in_specs=[SM, SM, HB],
        out_specs=(VM, VM),
        scratch_shapes=OWN,
        compiler_params=small(12),
        cost_estimate=BUSY,
        name="inner_rows" if along_rows else "inner_cols",
    )(*lists, own)


def outer(lists, lo, hi, kept, along_rows):
    _, _, one, two, whole = pl.pallas_call(
        functools.partial(outer_kernel, along_rows),
        out_shape=(EXT, ACC, EDGE, EDGE, FULL),
        in_specs=[SM, SM, HB, HB, VM, VM],
        out_specs=(VM, VM, VM, VM, HB),
        scratch_shapes=SIDES + [pltpu.SemaphoreType.DMA],
        input_output_aliases={4: 0, 5: 1},
        compiler_params=small(12),
        name="outer_rows" if along_rows else "outer_cols",
    )(*lists, lo, hi, *kept)
    return whole, one, two


def inner_last(lists, own):
    return pl.pallas_call(
        inner_last_kernel,
        out_shape=(EXT, ACC, RESULT),
        in_specs=[SM, SM, HB],
        out_specs=(VM, VM, HB),
        scratch_shapes=OWN + PARTS,
        compiler_params=small(12),
        cost_estimate=BUSY,
        name="inner_last",
    )(*lists, own)


def last(lists, lo, hi, kept):
    return pl.pallas_call(
        last_kernel,
        out_shape=(EXT, ACC, RESULT),
        in_specs=[SM, SM, HB, HB, VM, VM, HB],
        out_specs=(VM, VM, HB),
        scratch_shapes=SIDES + PARTS,
        input_output_aliases={4: 0, 5: 1, 6: 2},
        compiler_params=small(12),
        name="last",
    )(*lists, lo, hi, *kept)[2]


def beside(head, tail, axis):
    ends = lax.axis_size(axis) - 1
    lo = lax.ppermute(tail, axis, [(i, i + 1) for i in range(ends)])
    hi = lax.ppermute(head, axis, [(i + 1, i) for i in range(ends)])
    return lo, hi


def on_device(traces, destination, bin_index, dip_inline, dip_cross):
    x = traces.reshape(DEV, 4, 8, 128).transpose(0, 2, 1, 3).reshape(4096, 128)
    outgoing = pack(destination.reshape(-1), bin_index.T, x)
    arrived = lax.all_to_all(
        outgoing, ("inline", "crosslin"), split_axis=0, concat_axis=0, tiled=True
    )
    rows, cols = make_lists(dip_inline.reshape(-1), dip_cross.reshape(-1))
    bins = arrived[:, 64, 0, :8].astype(jnp.int32).reshape(-1)
    fold = jnp.sum(
        (jnp.arange(BINS, dtype=jnp.int32)[:, None] == bins[None, :]).astype(jnp.float32), axis=1
    )
    stacked, head, tail = put_bins(bins, 1.0 / jnp.maximum(fold, 1.0), rows[1], arrived)
    lo, hi = beside(head, tail, "inline")
    kept = inner(rows, stacked, True)
    first, left, right = outer(rows, lo, hi, kept, True)
    lo, hi = beside(left, right, "crosslin")
    kept = inner(cols, first, False)
    second, head, tail = outer(cols, lo, hi, kept, False)
    lo, hi = beside(head, tail, "inline")
    kept = inner_last(rows, second)
    return last(rows, lo, hi, kept)


def solution(mesh):
    return jax.shard_map(
        on_device,
        mesh=mesh,
        in_specs=(
            P(("inline", "crosslin"), None, None),
            P(("inline", "crosslin"), None),
            P(("inline", "crosslin"), None),
            P("inline", "crosslin"),
            P("inline", "crosslin"),
        ),
        out_specs=P("inline", "crosslin", None),
        check_vma=False,
    )
```

```python
import functools

import jax
import jax.numpy as jnp
from jax import lax
from jax.experimental import pallas as pl
from jax.experimental.pallas import tpu as pltpu
from jax.sharding import PartitionSpec as P

HALF = 7
DMAX = 2
DIPS = 2 * DMAX + 1
TILE = 32
BINS = TILE * TILE
DEV = 128
SUB, LANE = 8, 128
SPAN = 40
GROUP = 16
MORE = 4
ROOM = 18 * TILE + GROUP
PAY = 65
HALO = HALF * TILE

VM = pl.BlockSpec(memory_space=pltpu.VMEM)
SM = pl.BlockSpec(memory_space=pltpu.SMEM)
HB = pl.BlockSpec(memory_space=pl.ANY)


def params():
    return pltpu.CompilerParams(vmem_limit_bytes=60 << 20)


def pack_kernel(dest, bins, x, out, scr, z, brow, cnt, sem, bsem):
    for tr in range(4):
        for j in range(8):
            z[pl.ds(j * 128, 128), :] = x[pl.ds(j * 4 + tr, 128, stride=32), :].T
        for ti in range(SUB):
            scr[pl.ds(tr * 8 + ti, 128, stride=32), :] = z[pl.ds(ti, 128, stride=8), :].T
    brow[...] = jnp.full((DEV, 1, LANE), float(BINS), jnp.float32)

    def clear(i, _):
        cnt[i] = 0
        return 0

    lax.fori_loop(0, DEV, clear, 0, unroll=8)
    lane = lax.broadcasted_iota(jnp.int32, (1, LANE), 1)

    def place(b, _):
        t = dest[b]
        rank = cnt[t]
        cnt[t] = rank + 1
        pltpu.make_async_copy(
            scr.at[pl.ds(b * 32, 32)], out.at[t, pl.ds(rank * 32, 32), 0], sem
        ).start()
        row = brow[t]
        for q in range(4):
            row = jnp.where(lane == rank * 4 + q, bins[q, b].astype(jnp.float32), row)
        brow[t] = row
        return 0

    lax.fori_loop(0, DEV, place, 0)
    copy = pltpu.make_async_copy(brow, out.at[:, 64], bsem)
    copy.start()
    pltpu.make_async_copy(scr, scr, sem).wait()
    copy.wait()


def pack(dest, bins, x):
    return pl.pallas_call(
        pack_kernel,
        out_shape=jax.ShapeDtypeStruct((DEV, PAY, 1, LANE), jnp.float32),
        in_specs=[SM, SM, VM],
        out_specs=HB,
        scratch_shapes=[
            pltpu.VMEM((4096, LANE), jnp.float32),
            pltpu.VMEM((1024, LANE), jnp.float32),
            pltpu.VMEM((DEV, 1, LANE), jnp.float32),
            pltpu.SMEM((DEV,), jnp.int32),
            pltpu.SemaphoreType.DMA,
            pltpu.SemaphoreType.DMA,
        ],
        compiler_params=params(),
        name="pack",
    )(dest, bins, x)


def add_bin(dips, table, count, i, part):
    at = dips[i] + (part * DIPS + DMAX)
    n = count[at]
    table[n] = i
    count[at] = n + 1


def lists_kernel(along_rows, dips, table, count):
    for at in range(2 * DIPS):
        count[at] = at * ROOM
    inside = range(HALF, TILE - HALF)
    if along_rows:
        for low, high, part in ((0, HALF, 1), (HALF, TILE - HALF, 0), (TILE - HALF, TILE, 1)):

            def add(i, _):
                add_bin(dips, table, count, i, part)
                return 0

            lax.fori_loop(low * TILE, high * TILE, add, 0, unroll=16)
    else:

        def row(r, _):
            for c in range(TILE):
                add_bin(dips, table, count, r * TILE + c, 0 if c in inside else 1)
            return 0

        lax.fori_loop(0, TILE, row, 0)
    for at in range(2 * DIPS):
        n = count[at]
        for u in range(GROUP):
            table[n + u] = BINS
        count[at] = n - at * ROOM


def both_lists_kernel(dip_rows, dip_cols, table_rows, count_rows, table_cols, count_cols):
    lists_kernel(True, dip_rows, table_rows, count_rows)
    lists_kernel(False, dip_cols, table_cols, count_cols)


def make_lists(dip_rows, dip_cols):
    table = jax.ShapeDtypeStruct((2 * DIPS * ROOM,), jnp.int32)
    count = jax.ShapeDtypeStruct((2 * DIPS,), jnp.int32)
    table_rows, count_rows, table_cols, count_cols = pl.pallas_call(
        both_lists_kernel,
        out_shape=(table, count, table, count),
        in_specs=[SM, SM],
        out_specs=(SM,) * 4,
        compiler_params=params(),
        cost_estimate=pl.CostEstimate(flops=0, bytes_accessed=24 << 20, transcendentals=0),
        name="lists",
    )(dip_rows, dip_cols)
    return (table_rows, count_rows), (table_cols, count_cols)


def bin_kernel(bins, scale, after, x_hbm, out, head, tail, x, sems, *sums):
    chunk = DEV // MORE
    copies = [
        pltpu.make_async_copy(
            x_hbm.at[pl.ds(q * chunk, chunk), pl.ds(0, 64), 0], x.at[pl.ds(q * chunk, chunk)], sems.at[q]
        )
        for q in range(MORE)
    ]
    for copy in copies:
        copy.start()
    zero = jnp.zeros((SUB, LANE), jnp.float32)

    def clear(i, _):
        for s in sums:
            s[i] = zero
        return 0

    lax.fori_loop(0, BINS, clear, 0, unroll=8)

    def add(i, _):
        for slot in range(2):
            for tr in range(4):
                b = bins[i * 8 + slot * 4 + tr]
                sums[tr][b] += x[i, pl.ds(slot * 32 + tr * 8, 8), :]
        return 0

    for q in range(MORE):
        copies[q].wait()
        lax.fori_loop(q * chunk, (q + 1) * chunk, add, 0, unroll=2)

    def finish(i, _):
        out[i] = ((sums[0][i] + sums[1][i]) + (sums[2][i] + sums[3][i])) * scale[i]
        return 0

    lax.fori_loop(0, BINS, finish, 0, unroll=8)
    head[...] = out[pl.ds(0, HALO)]
    tail[...] = out[pl.ds(BINS - HALO, HALO)]


FULL = jax.ShapeDtypeStruct((BINS, SUB, LANE), jnp.float32)
EDGE = jax.ShapeDtypeStruct((HALO, SUB, LANE), jnp.float32)


def put_bins(bins, scale, after, x):
    return pl.pallas_call(
        bin_kernel,
        out_shape=(FULL, EDGE, EDGE),
        in_specs=[SM, SM, SM, HB],
        out_specs=(VM, VM, VM),
        scratch_shapes=[
            pltpu.VMEM((DEV, 64, LANE), jnp.float32),
            pltpu.SemaphoreType.DMA((MORE,)),
            *[pltpu.VMEM((BINS + 1, SUB, LANE), jnp.float32) for _ in range(4)],
        ],
        compiler_params=small(58),
        name="put_bins",
    )(bins, scale, after, x)


def shift_matrix():
    k = lax.broadcasted_iota(jnp.int32, (2 * LANE, 4 * LANE), 0) % LANE
    n = lax.broadcasted_iota(jnp.int32, (2 * LANE, 4 * LANE), 1)
    block = n // LANE
    move = jnp.where(block < 2, block - 2, block - 1)
    return jnp.where(k == n % LANE + move, 1.0, 0.0).astype(jnp.bfloat16)


def widen(ext, starts, x, mat):
    n = x.shape[0]
    flat = x.reshape(n * SUB, LANE)
    high = flat.astype(jnp.bfloat16)
    low = (flat - high.astype(jnp.float32)).astype(jnp.bfloat16)
    moved = jnp.dot(
        jnp.concatenate([high, low], axis=1), mat[...], preferred_element_type=jnp.float32
    )
    for u in range(n):
        at = starts[u]
        ext[pl.ds(at + 16, 8), :] = flat[u * 8 : u * 8 + 8]
        for block, offset in enumerate((0, 8, 24, 32)):
            ext[pl.ds(at + offset, 8), :] = moved[
                u * 8 : u * 8 + 8, block * LANE : (block + 1) * LANE
            ]


WIDE = TILE + 2 * HALF
ROW_PITCH = TILE * SPAN + 8
COL_PITCH = SPAN
EXT_ROWS = 72000


def start_of(b, along_rows):
    if along_rows:
        return b * SPAN + 8 * (b >> 5)
    return (b + 2 * HALF * (b >> 5)) * SPAN


def inner_margins(ext, own_hbm, own, sems, mat, along_rows):
    mat[...] = shift_matrix()
    shift = HALF * (ROW_PITCH if along_rows else COL_PITCH)
    chunk = BINS // MORE
    copies = [
        pltpu.make_async_copy(
            own_hbm.at[pl.ds(q * chunk, chunk)], own.at[pl.ds(q * chunk, chunk)], sems.at[q]
        )
        for q in range(MORE)
    ]
    for copy in copies:
        copy.start()

    below = ROW_PITCH if along_rows else WIDE * SPAN

    def two_rows(r, _):
        first = start_of(r * 2 * TILE, along_rows) + shift
        starts = [
            pl.multiple_of(first + p * below + c * SPAN, 8) for p in range(2) for c in range(TILE)
        ]
        widen(ext, starts, own[pl.ds(r * 2 * TILE, 2 * TILE)], mat)
        return 0

    for q in range(MORE):
        copies[q].wait()
        lax.fori_loop(q * TILE // MORE // 2, (q + 1) * TILE // MORE // 2, two_rows, 0)


def outer_margins(ext, lo_hbm, hi_hbm, lo, hi, sems, mat, along_rows):
    copies = [
        pltpu.make_async_copy(lo_hbm, lo, sems.at[0]),
        pltpu.make_async_copy(hi_hbm, hi, sems.at[1]),
    ]
    for copy in copies:
        copy.start()
    mat[...] = shift_matrix()
    for copy in copies:
        copy.wait()
    far = TILE + HALF
    if along_rows:

        def row(r, _):
            starts = [
                pl.multiple_of((r + beyond) * ROW_PITCH + c * SPAN, 8)
                for beyond in (0, far)
                for c in range(TILE)
            ]
            here = pl.ds(r * TILE, TILE)
            widen(ext, starts, jnp.concatenate([lo[here], hi[here]], axis=0), mat)
            return 0

        lax.fori_loop(0, HALF, row, 0)
    else:

        def four_rows(q, _):
            starts = [
                pl.multiple_of(((q * 4 + p) * WIDE + beyond + c) * SPAN, 8)
                for beyond in (0, far)
                for p in range(4)
                for c in range(HALF)
            ]
            here = pl.ds(q * 4 * HALF, 4 * HALF)
            widen(ext, starts, jnp.concatenate([lo[here], hi[here]], axis=0), mat)
            return 0

        lax.fori_loop(0, TILE // 4, four_rows, 0)


def steer(table, count, part, ext, along_rows, acc):
    pitch = ROW_PITCH if along_rows else COL_PITCH
    for d in range(-DMAX, DMAX + 1):
        at = part * DIPS + d + DMAX

        def group(g, _):
            for u in range(GROUP):
                b = table[at * ROOM + g * GROUP + u]
                first = pl.multiple_of(start_of(b, along_rows), 8)
                view = ext.at[pl.ds(first, 14 * pitch + SPAN)]

                def tap(k):
                    return view[pl.ds(16 + (k + HALF) * pitch + d * k, 8), :]

                total = tap(0) * (1.0 / 8.0)
                for k in range(1, HALF + 1):
                    total = total + (tap(k) + tap(-k)) * ((HALF + 1 - k) / 64.0)
                acc[b] = total
            return 0

        lax.fori_loop(0, (count[at] + GROUP - 1) // GROUP, group, 0)


def inner_kernel(along_rows, table, count, own_hbm, ext, acc, own, sems, mat):
    inner_margins(ext, own_hbm, own, sems, mat, along_rows)
    steer(table, count, 0, ext, along_rows, acc)


def outer_kernel(
    along_rows, table, count, lo_hbm, hi_hbm, ext_in, acc_in,
    ext, acc, one, two, whole, lo, hi, sems, mat, away,
):
    outer_margins(ext, lo_hbm, hi_hbm, lo, hi, sems, mat, along_rows)
    steer(table, count, 1, ext, along_rows, acc)
    keep = pltpu.make_async_copy(acc.at[pl.ds(0, BINS)], whole, away)
    keep.start()
    if along_rows:

        def cut(r, _):
            for c in range(HALF):
                one[r * HALF + c] = acc[r * TILE + c]
                two[r * HALF + c] = acc[r * TILE + TILE - HALF + c]
            return 0

        lax.fori_loop(0, TILE, cut, 0)
    else:
        one[...] = acc[pl.ds(0, HALO)]
        two[...] = acc[pl.ds(BINS - HALO, HALO)]
    keep.wait()


def natural(acc, out_hbm, z, parts, sems, groups):
    copies = []
    for slot, i in enumerate(groups):
        for ti in range(SUB):
            z[pl.ds(ti, 128, stride=8), :] = acc[pl.ds(i * 128, 128), ti, :].T
        for j in range(8):
            parts[slot, :, :, pl.ds(j * 128, 128)] = (
                z[pl.ds(j * 128, 128), :].T.reshape(4, TILE, 128)
            )
        copy = pltpu.make_async_copy(parts.at[slot], out_hbm.at[pl.ds(i * 4, 4)], sems.at[slot])
        copy.start()
        copies.append(copy)
    for copy in copies:
        copy.wait()


def inner_last_kernel(table, count, own_hbm, ext, acc, out_hbm, own, sems, mat, z, parts, outs):
    inner_kernel(True, table, count, own_hbm, ext, acc, own, sems, mat)
    natural(acc, out_hbm, z, parts, outs, (2, 3, 4, 5))


def last_kernel(
    table, count, lo_hbm, hi_hbm, ext_in, acc_in, out_in, ext, acc, out_hbm,
    lo, hi, sems, mat, z, parts, outs,
):
    outer_margins(ext, lo_hbm, hi_hbm, lo, hi, sems, mat, True)
    steer(table, count, 1, ext, True, acc)
    natural(acc, out_hbm, z, parts, outs, (0, 1, 6, 7))


EXT = pltpu.VMEM((EXT_ROWS, LANE), jnp.float32)
ACC = pltpu.VMEM((BINS + 1, SUB, LANE), jnp.float32)


def small(mib):
    return pltpu.CompilerParams(vmem_limit_bytes=mib << 20)


OWN = [
    pltpu.VMEM((BINS, SUB, LANE), jnp.float32),
    pltpu.SemaphoreType.DMA((MORE,)),
    pltpu.VMEM((2 * LANE, 4 * LANE), jnp.bfloat16),
]
SIDES = [
    pltpu.VMEM((HALO, SUB, LANE), jnp.float32),
    pltpu.VMEM((HALO, SUB, LANE), jnp.float32),
    pltpu.SemaphoreType.DMA((2,)),
    pltpu.VMEM((2 * LANE, 4 * LANE), jnp.bfloat16),
]
PARTS = [
    pltpu.VMEM((1024, LANE), jnp.float32),
    pltpu.VMEM((4, 4, TILE, SUB * LANE), jnp.float32),
    pltpu.SemaphoreType.DMA((4,)),
]
RESULT = jax.ShapeDtypeStruct((TILE, TILE, SUB * LANE), jnp.float32)
BUSY = pl.CostEstimate(flops=0, bytes_accessed=48 << 20, transcendentals=0)


def inner(lists, own, along_rows):
    return pl.pallas_call(
        functools.partial(inner_kernel, along_rows),
        out_shape=(EXT, ACC),
        in_specs=[SM, SM, HB],
        out_specs=(VM, VM),
        scratch_shapes=OWN,
        compiler_params=small(12),
        cost_estimate=BUSY,
        name="inner_rows" if along_rows else "inner_cols",
    )(*lists, own)


def outer(lists, lo, hi, kept, along_rows):
    _, _, one, two, whole = pl.pallas_call(
        functools.partial(outer_kernel, along_rows),
        out_shape=(EXT, ACC, EDGE, EDGE, FULL),
        in_specs=[SM, SM, HB, HB, VM, VM],
        out_specs=(VM, VM, VM, VM, HB),
        scratch_shapes=SIDES + [pltpu.SemaphoreType.DMA],
        input_output_aliases={4: 0, 5: 1},
        compiler_params=small(12),
        name="outer_rows" if along_rows else "outer_cols",
    )(*lists, lo, hi, *kept)
    return whole, one, two


def inner_last(lists, own):
    return pl.pallas_call(
        inner_last_kernel,
        out_shape=(EXT, ACC, RESULT),
        in_specs=[SM, SM, HB],
        out_specs=(VM, VM, HB),
        scratch_shapes=OWN + PARTS,
        compiler_params=small(12),
        cost_estimate=BUSY,
        name="inner_last",
    )(*lists, own)


def last(lists, lo, hi, kept):
    return pl.pallas_call(
        last_kernel,
        out_shape=(EXT, ACC, RESULT),
        in_specs=[SM, SM, HB, HB, VM, VM, HB],
        out_specs=(VM, VM, HB),
        scratch_shapes=SIDES + PARTS,
        input_output_aliases={4: 0, 5: 1, 6: 2},
        compiler_params=small(12),
        name="last",
    )(*lists, lo, hi, *kept)[2]


def beside(head, tail, axis):
    ends = lax.axis_size(axis) - 1
    lo = lax.ppermute(tail, axis, [(i, i + 1) for i in range(ends)])
    hi = lax.ppermute(head, axis, [(i + 1, i) for i in range(ends)])
    return lo, hi


def on_device(traces, destination, bin_index, dip_inline, dip_cross):
    x = traces.reshape(DEV, 4, 8, 128).transpose(0, 2, 1, 3).reshape(4096, 128)
    outgoing = pack(destination.reshape(-1), bin_index.T, x)
    arrived = lax.all_to_all(
        outgoing, ("inline", "crosslin"), split_axis=0, concat_axis=0, tiled=True
    )
    rows, cols = make_lists(dip_inline.reshape(-1), dip_cross.reshape(-1))
    bins = arrived[:, 64, 0, :8].astype(jnp.int32).reshape(-1)
    fold = jnp.sum(
        (jnp.arange(BINS, dtype=jnp.int32)[:, None] == bins[None, :]).astype(jnp.float32), axis=1
    )
    stacked, head, tail = put_bins(bins, 1.0 / jnp.maximum(fold, 1.0), rows[1], arrived)
    lo, hi = beside(head, tail, "inline")
    kept = inner(rows, stacked, True)
    first, left, right = outer(rows, lo, hi, kept, True)
    lo, hi = beside(left, right, "crosslin")
    kept = inner(cols, first, False)
    second, head, tail = outer(cols, lo, hi, kept, False)
    lo, hi = beside(head, tail, "inline")
    kept = inner_last(rows, second)
    return last(rows, lo, hi, kept)


def solution(mesh):
    return jax.shard_map(
        on_device,
        mesh=mesh,
        in_specs=(
            P(("inline", "crosslin"), None, None),
            P(("inline", "crosslin"), None),
            P(("inline", "crosslin"), None),
            P("inline", "crosslin"),
            P("inline", "crosslin"),
        ),
        out_specs=P("inline", "crosslin", None),
        check_vma=False,
    )
```

```python
import functools

import jax
import jax.numpy as jnp
from jax import lax
from jax.experimental import pallas as pl
from jax.experimental.pallas import tpu as pltpu
from jax.sharding import PartitionSpec as P

HALF = 7
DMAX = 2
DIPS = 2 * DMAX + 1
TILE = 32
BINS = TILE * TILE
DEV = 128
SUB, LANE = 8, 128
SPAN = 40
GROUP = 16
MORE = 4
ROOM = 18 * TILE + GROUP
PAY = 65
HALO = HALF * TILE

VM = pl.BlockSpec(memory_space=pltpu.VMEM)
SM = pl.BlockSpec(memory_space=pltpu.SMEM)
HB = pl.BlockSpec(memory_space=pl.ANY)


def params():
    return pltpu.CompilerParams(vmem_limit_bytes=60 << 20)


def pack_kernel(dest, bins, x, out, scr, z, brow, cnt, sem, bsem):
    for tr in range(4):
        for j in range(8):
            z[pl.ds(j * 128, 128), :] = x[pl.ds(j * 4 + tr, 128, stride=32), :].T
        for ti in range(SUB):
            scr[pl.ds(tr * 8 + ti, 128, stride=32), :] = z[pl.ds(ti, 128, stride=8), :].T
    brow[...] = jnp.full((DEV, 1, LANE), float(BINS), jnp.float32)

    def clear(i, _):
        cnt[i] = 0
        return 0

    lax.fori_loop(0, DEV, clear, 0, unroll=8)
    lane = lax.broadcasted_iota(jnp.int32, (1, LANE), 1)

    def place(b, _):
        t = dest[b]
        rank = cnt[t]
        cnt[t] = rank + 1
        pltpu.make_async_copy(
            scr.at[pl.ds(b * 32, 32)], out.at[t, pl.ds(rank * 32, 32), 0], sem
        ).start()
        row = brow[t]
        for q in range(4):
            row = jnp.where(lane == rank * 4 + q, bins[q, b].astype(jnp.float32), row)
        brow[t] = row
        return 0

    lax.fori_loop(0, DEV, place, 0)
    copy = pltpu.make_async_copy(brow, out.at[:, 64], bsem)
    copy.start()
    pltpu.make_async_copy(scr, scr, sem).wait()
    copy.wait()


def pack(dest, bins, x):
    return pl.pallas_call(
        pack_kernel,
        out_shape=jax.ShapeDtypeStruct((DEV, PAY, 1, LANE), jnp.float32),
        in_specs=[SM, SM, VM],
        out_specs=HB,
        scratch_shapes=[
            pltpu.VMEM((4096, LANE), jnp.float32),
            pltpu.VMEM((1024, LANE), jnp.float32),
            pltpu.VMEM((DEV, 1, LANE), jnp.float32),
            pltpu.SMEM((DEV,), jnp.int32),
            pltpu.SemaphoreType.DMA,
            pltpu.SemaphoreType.DMA,
        ],
        compiler_params=params(),
        name="pack",
    )(dest, bins, x)


def add_bin(dips, table, count, i, part):
    at = dips[i] + (part * DIPS + DMAX)
    n = count[at]
    table[n] = i
    count[at] = n + 1


def lists_kernel(along_rows, dips, table, count):
    for at in range(2 * DIPS):
        count[at] = at * ROOM
    inside = range(HALF, TILE - HALF)
    if along_rows:
        for low, high, part in ((0, HALF, 1), (HALF, TILE - HALF, 0), (TILE - HALF, TILE, 1)):

            def add(i, _):
                add_bin(dips, table, count, i, part)
                return 0

            lax.fori_loop(low * TILE, high * TILE, add, 0, unroll=16)
    else:

        def row(r, _):
            for c in range(TILE):
                add_bin(dips, table, count, r * TILE + c, 0 if c in inside else 1)
            return 0

        lax.fori_loop(0, TILE, row, 0)
    for at in range(2 * DIPS):
        n = count[at]
        for u in range(GROUP):
            table[n + u] = BINS
        count[at] = n - at * ROOM


def both_lists_kernel(dip_rows, dip_cols, table_rows, count_rows, table_cols, count_cols):
    lists_kernel(True, dip_rows, table_rows, count_rows)
    lists_kernel(False, dip_cols, table_cols, count_cols)


def make_lists(dip_rows, dip_cols):
    table = jax.ShapeDtypeStruct((2 * DIPS * ROOM,), jnp.int32)
    count = jax.ShapeDtypeStruct((2 * DIPS,), jnp.int32)
    table_rows, count_rows, table_cols, count_cols = pl.pallas_call(
        both_lists_kernel,
        out_shape=(table, count, table, count),
        in_specs=[SM, SM],
        out_specs=(SM,) * 4,
        compiler_params=params(),
        cost_estimate=pl.CostEstimate(flops=0, bytes_accessed=24 << 20, transcendentals=0),
        name="lists",
    )(dip_rows, dip_cols)
    return (table_rows, count_rows), (table_cols, count_cols)


def bin_kernel(bins, scale, after, x_hbm, out, head, tail, x, sems, *sums):
    chunk = DEV // MORE
    copies = [
        pltpu.make_async_copy(
            x_hbm.at[pl.ds(q * chunk, chunk), pl.ds(0, 64), 0], x.at[pl.ds(q * chunk, chunk)], sems.at[q]
        )
        for q in range(MORE)
    ]
    for copy in copies:
        copy.start()
    zero = jnp.zeros((SUB, LANE), jnp.float32)

    def clear(i, _):
        for s in sums:
            s[i] = zero
        return 0

    lax.fori_loop(0, BINS, clear, 0, unroll=8)

    def add(i, _):
        for slot in range(2):
            for tr in range(4):
                b = bins[i * 8 + slot * 4 + tr]
                sums[tr][b] += x[i, pl.ds(slot * 32 + tr * 8, 8), :]
        return 0

    for q in range(MORE):
        copies[q].wait()
        lax.fori_loop(q * chunk, (q + 1) * chunk, add, 0, unroll=2)

    def finish(i, _):
        out[i] = ((sums[0][i] + sums[1][i]) + (sums[2][i] + sums[3][i])) * scale[i]
        return 0

    lax.fori_loop(0, BINS, finish, 0, unroll=8)
    head[...] = out[pl.ds(0, HALO)]
    tail[...] = out[pl.ds(BINS - HALO, HALO)]


FULL = jax.ShapeDtypeStruct((BINS, SUB, LANE), jnp.float32)
EDGE = jax.ShapeDtypeStruct((HALO, SUB, LANE), jnp.float32)


def put_bins(bins, scale, after, x):
    return pl.pallas_call(
        bin_kernel,
        out_shape=(FULL, EDGE, EDGE),
        in_specs=[SM, SM, SM, HB],
        out_specs=(VM, VM, VM),
        scratch_shapes=[
            pltpu.VMEM((DEV, 64, LANE), jnp.float32),
            pltpu.SemaphoreType.DMA((MORE,)),
            *[pltpu.VMEM((BINS + 1, SUB, LANE), jnp.float32) for _ in range(4)],
        ],
        compiler_params=small(58),
        name="put_bins",
    )(bins, scale, after, x)


def shift_matrix():
    k = lax.broadcasted_iota(jnp.int32, (2 * LANE, 4 * LANE), 0) % LANE
    n = lax.broadcasted_iota(jnp.int32, (2 * LANE, 4 * LANE), 1)
    block = n // LANE
    move = jnp.where(block < 2, block - 2, block - 1)
    return jnp.where(k == n % LANE + move, 1.0, 0.0).astype(jnp.bfloat16)


def widen(ext, starts, x, mat):
    n = x.shape[0]
    flat = x.reshape(n * SUB, LANE)
    high = flat.astype(jnp.bfloat16)
    low = (flat - high.astype(jnp.float32)).astype(jnp.bfloat16)
    moved = jnp.dot(
        jnp.concatenate([high, low], axis=1), mat[...], preferred_element_type=jnp.float32
    )
    for u in range(n):
        at = starts[u]
        ext[pl.ds(at + 16, 8), :] = flat[u * 8 : u * 8 + 8]
        for block, offset in enumerate((0, 8, 24, 32)):
            ext[pl.ds(at + offset, 8), :] = moved[
                u * 8 : u * 8 + 8, block * LANE : (block + 1) * LANE
            ]


WIDE = TILE + 2 * HALF
ROW_PITCH = TILE * SPAN + 8
COL_PITCH = SPAN
EXT_ROWS = 70000


def start_of(b, along_rows):
    if along_rows:
        return b * SPAN + 8 * (b >> 5)
    return (b + 2 * HALF * (b >> 5)) * SPAN


def inner_margins(ext, own_hbm, own, sems, mat, along_rows):
    mat[...] = shift_matrix()
    shift = HALF * (ROW_PITCH if along_rows else COL_PITCH)
    chunk = BINS // MORE
    copies = [
        pltpu.make_async_copy(
            own_hbm.at[pl.ds(q * chunk, chunk)], own.at[pl.ds(q * chunk, chunk)], sems.at[q]
        )
        for q in range(MORE)
    ]
    for copy in copies:
        copy.start()

    below = ROW_PITCH if along_rows else WIDE * SPAN

    def two_rows(r, _):
        first = start_of(r * 2 * TILE, along_rows) + shift
        starts = [
            pl.multiple_of(first + p * below + c * SPAN, 8) for p in range(2) for c in range(TILE)
        ]
        widen(ext, starts, own[pl.ds(r * 2 * TILE, 2 * TILE)], mat)
        return 0

    for q in range(MORE):
        copies[q].wait()
        lax.fori_loop(q * TILE // MORE // 2, (q + 1) * TILE // MORE // 2, two_rows, 0)


def outer_margins(ext, lo_hbm, hi_hbm, lo, hi, sems, mat, along_rows):
    copies = [
        pltpu.make_async_copy(lo_hbm, lo, sems.at[0]),
        pltpu.make_async_copy(hi_hbm, hi, sems.at[1]),
    ]
    for copy in copies:
        copy.start()
    mat[...] = shift_matrix()
    for copy in copies:
        copy.wait()
    far = TILE + HALF
    if along_rows:

        def row(r, _):
            starts = [
                pl.multiple_of((r + beyond) * ROW_PITCH + c * SPAN, 8)
                for beyond in (0, far)
                for c in range(TILE)
            ]
            here = pl.ds(r * TILE, TILE)
            widen(ext, starts, jnp.concatenate([lo[here], hi[here]], axis=0), mat)
            return 0

        lax.fori_loop(0, HALF, row, 0)
    else:

        def four_rows(q, _):
            starts = [
                pl.multiple_of(((q * 4 + p) * WIDE + beyond + c) * SPAN, 8)
                for beyond in (0, far)
                for p in range(4)
                for c in range(HALF)
            ]
            here = pl.ds(q * 4 * HALF, 4 * HALF)
            widen(ext, starts, jnp.concatenate([lo[here], hi[here]], axis=0), mat)
            return 0

        lax.fori_loop(0, TILE // 4, four_rows, 0)


def steer(table, count, part, ext, along_rows, acc):
    pitch = ROW_PITCH if along_rows else COL_PITCH
    for d in range(-DMAX, DMAX + 1):
        at = part * DIPS + d + DMAX

        def group(g, _):
            for u in range(GROUP):
                b = table[at * ROOM + g * GROUP + u]
                first = pl.multiple_of(start_of(b, along_rows), 8)
                view = ext.at[pl.ds(first, 14 * pitch + SPAN)]

                def tap(k):
                    return view[pl.ds(16 + (k + HALF) * pitch + d * k, 8), :]

                total = tap(0) * (1.0 / 8.0)
                for k in range(1, HALF + 1):
                    total = total + (tap(k) + tap(-k)) * ((HALF + 1 - k) / 64.0)
                acc[b] = total
            return 0

        lax.fori_loop(0, (count[at] + GROUP - 1) // GROUP, group, 0)


def inner_kernel(along_rows, table, count, own_hbm, ext, acc, own, sems, mat):
    inner_margins(ext, own_hbm, own, sems, mat, along_rows)
    steer(table, count, 0, ext, along_rows, acc)


def outer_kernel(
    along_rows, table, count, lo_hbm, hi_hbm, ext_in, acc_in,
    ext, acc, one, two, whole, lo, hi, sems, mat, away,
):
    outer_margins(ext, lo_hbm, hi_hbm, lo, hi, sems, mat, along_rows)
    steer(table, count, 1, ext, along_rows, acc)
    keep = pltpu.make_async_copy(acc.at[pl.ds(0, BINS)], whole, away)
    keep.start()
    if along_rows:

        def cut(r, _):
            for c in range(HALF):
                one[r * HALF + c] = acc[r * TILE + c]
                two[r * HALF + c] = acc[r * TILE + TILE - HALF + c]
            return 0

        lax.fori_loop(0, TILE, cut, 0)
    else:
        one[...] = acc[pl.ds(0, HALO)]
        two[...] = acc[pl.ds(BINS - HALO, HALO)]
    keep.wait()


def natural(acc, out_hbm, z, parts, sems, groups):
    copies = []
    for slot, i in enumerate(groups):
        for ti in range(SUB):
            z[pl.ds(ti, 128, stride=8), :] = acc[pl.ds(i * 128, 128), ti, :].T
        for j in range(8):
            parts[slot, :, :, pl.ds(j * 128, 128)] = (
                z[pl.ds(j * 128, 128), :].T.reshape(4, TILE, 128)
            )
        copy = pltpu.make_async_copy(parts.at[slot], out_hbm.at[pl.ds(i * 4, 4)], sems.at[slot])
        copy.start()
        copies.append(copy)
    for copy in copies:
        copy.wait()


def inner_last_kernel(table, count, own_hbm, ext, acc, out_hbm, own, sems, mat, z, parts, outs):
    inner_kernel(True, table, count, own_hbm, ext, acc, own, sems, mat)
    natural(acc, out_hbm, z, parts, outs, (2, 3, 4, 5))


def last_kernel(
    table, count, lo_hbm, hi_hbm, ext_in, acc_in, out_in, ext, acc, out_hbm,
    lo, hi, sems, mat, z, parts, outs,
):
    outer_margins(ext, lo_hbm, hi_hbm, lo, hi, sems, mat, True)
    steer(table, count, 1, ext, True, acc)
    natural(acc, out_hbm, z, parts, outs, (0, 1, 6, 7))


EXT = pltpu.VMEM((EXT_ROWS, LANE), jnp.float32)
ACC = pltpu.VMEM((BINS + 1, SUB, LANE), jnp.float32)


def small(mib):
    return pltpu.CompilerParams(vmem_limit_bytes=mib << 20)


OWN = [
    pltpu.VMEM((BINS, SUB, LANE), jnp.float32),
    pltpu.SemaphoreType.DMA((MORE,)),
    pltpu.VMEM((2 * LANE, 4 * LANE), jnp.bfloat16),
]
SIDES = [
    pltpu.VMEM((HALO, SUB, LANE), jnp.float32),
    pltpu.VMEM((HALO, SUB, LANE), jnp.float32),
    pltpu.SemaphoreType.DMA((2,)),
    pltpu.VMEM((2 * LANE, 4 * LANE), jnp.bfloat16),
]
PARTS = [
    pltpu.VMEM((1024, LANE), jnp.float32),
    pltpu.VMEM((4, 4, TILE, SUB * LANE), jnp.float32),
    pltpu.SemaphoreType.DMA((4,)),
]
RESULT = jax.ShapeDtypeStruct((TILE, TILE, SUB * LANE), jnp.float32)
BUSY = pl.CostEstimate(flops=0, bytes_accessed=48 << 20, transcendentals=0)


def inner(lists, own, along_rows):
    return pl.pallas_call(
        functools.partial(inner_kernel, along_rows),
        out_shape=(EXT, ACC),
        in_specs=[SM, SM, HB],
        out_specs=(VM, VM),
        scratch_shapes=OWN,
        compiler_params=small(12),
        cost_estimate=BUSY,
        name="inner_rows" if along_rows else "inner_cols",
    )(*lists, own)


def outer(lists, lo, hi, kept, along_rows):
    _, _, one, two, whole = pl.pallas_call(
        functools.partial(outer_kernel, along_rows),
        out_shape=(EXT, ACC, EDGE, EDGE, FULL),
        in_specs=[SM, SM, HB, HB, VM, VM],
        out_specs=(VM, VM, VM, VM, HB),
        scratch_shapes=SIDES + [pltpu.SemaphoreType.DMA],
        input_output_aliases={4: 0, 5: 1},
        compiler_params=small(12),
        name="outer_rows" if along_rows else "outer_cols",
    )(*lists, lo, hi, *kept)
    return whole, one, two


def inner_last(lists, own):
    return pl.pallas_call(
        inner_last_kernel,
        out_shape=(EXT, ACC, RESULT),
        in_specs=[SM, SM, HB],
        out_specs=(VM, VM, HB),
        scratch_shapes=OWN + PARTS,
        compiler_params=small(12),
        cost_estimate=BUSY,
        name="inner_last",
    )(*lists, own)


def last(lists, lo, hi, kept):
    return pl.pallas_call(
        last_kernel,
        out_shape=(EXT, ACC, RESULT),
        in_specs=[SM, SM, HB, HB, VM, VM, HB],
        out_specs=(VM, VM, HB),
        scratch_shapes=SIDES + PARTS,
        input_output_aliases={4: 0, 5: 1, 6: 2},
        compiler_params=small(12),
        name="last",
    )(*lists, lo, hi, *kept)[2]


def beside(head, tail, axis):
    ends = lax.axis_size(axis) - 1
    lo = lax.ppermute(tail, axis, [(i, i + 1) for i in range(ends)])
    hi = lax.ppermute(head, axis, [(i + 1, i) for i in range(ends)])
    return lo, hi


def on_device(traces, destination, bin_index, dip_inline, dip_cross):
    x = traces.reshape(DEV, 4, 8, 128).transpose(0, 2, 1, 3).reshape(4096, 128)
    outgoing = pack(destination.reshape(-1), bin_index.T, x)
    arrived = lax.all_to_all(
        outgoing, ("inline", "crosslin"), split_axis=0, concat_axis=0, tiled=True
    )
    rows, cols = make_lists(dip_inline.reshape(-1), dip_cross.reshape(-1))
    bins = arrived[:, 64, 0, :8].astype(jnp.int32).reshape(-1)
    fold = jnp.sum(
        (jnp.arange(BINS, dtype=jnp.int32)[:, None] == bins[None, :]).astype(jnp.float32), axis=1
    )
    stacked, head, tail = put_bins(bins, 1.0 / jnp.maximum(fold, 1.0), rows[1], arrived)
    lo, hi = beside(head, tail, "inline")
    kept = inner(rows, stacked, True)
    first, left, right = outer(rows, lo, hi, kept, True)
    lo, hi = beside(left, right, "crosslin")
    kept = inner(cols, first, False)
    second, head, tail = outer(cols, lo, hi, kept, False)
    lo, hi = beside(head, tail, "inline")
    kept = inner_last(rows, second)
    return last(rows, lo, hi, kept)


def solution(mesh):
    return jax.shard_map(
        on_device,
        mesh=mesh,
        in_specs=(
            P(("inline", "crosslin"), None, None),
            P(("inline", "crosslin"), None),
            P(("inline", "crosslin"), None),
            P("inline", "crosslin"),
            P("inline", "crosslin"),
        ),
        out_specs=P("inline", "crosslin", None),
        check_vma=False,
    )
```
